32 devices in a mesh: gx: 8 (over z, y), gy: 4 (over x, core).
Axes of the slice: x: 2, y: 2, z: 4, core: 2. Of those that a mesh axis runs over, the one named last changes fastest.
Arguments:
- right_hand: float32 [4, 6, 32, 1536], P(None, None, 'gx', 'gy'), may hold values from -40 to 40
- region_labels: int32 [32, 1536], P('gx', 'gy'), may hold values from 0 to 2
- potential_table: float32 [3, 6], replicated, may hold values from 0.5 to 3
- coupling: float32 [3, 6, 6], replicated, may hold values from -0.1 to 1, as said below
- aggregate_map: int32 [8, 96], P('gx', 'gy'), may hold values from 0 to 63
- coarse_inverse: float32 [384, 384], replicated, may hold values from -0.2 to 2
Outputs:
- solution: float32 [4, 6, 32, 1536], P(None, None, 'gx', 'gy')
The draws below stay inside these ranges and needn't reach their ends.
Inputs may be any that keep to these rules, and one draw needn't show every extreme that they name: `coupling`: symmetric in the two band indices.
All inputs are finite; a program needn't handle non-finite values.
Results may differ from the reference program's by a relative error of at most 0.0003.
Values sent between devices are 32-bit elements; how exact they have to be, the bound alone decides.
No kernel may reach another device: no remote copies, remote signals or barrier semaphores. Data moves between devices by JAX's collectives and lax.ppermute only.
A program may use at most 64 MiB of HBM per device.

```python
import math
import jax
import jax.numpy as jnp
from jax import lax

NZ = 48
BANDS = 6
VECS = 4
REGIONS = 3
ITERS = 3
LEVELS = 3
NAGG = 64
NX = 32
NY = 32
AGG_CELLS = 12


def draw_right_hand(key, part):
    first, second = jax.random.split(key)
    scales = jnp.exp(jax.random.uniform(first, (1, BANDS, NX, 1), jnp.float32) * math.log(10.0))
    noise = jnp.clip(jax.random.normal(second, (VECS, BANDS, NX, NY * NZ), jnp.float32), -4.0, 4.0)
    return scales * noise


def draw_coupling(key, part):
    first, second = jax.random.split(key)
    diagonal_part = jnp.exp(jax.random.uniform(first, (3, BANDS), jnp.float32, math.log(0.3), 0.0))
    off_part = jax.random.uniform(second, (3, BANDS, BANDS), jnp.float32, -0.1, 0.1)
    off_part = 0.5 * (off_part + jnp.swapaxes(off_part, 1, 2))
    identity = jnp.eye(BANDS, dtype=jnp.float32)
    return off_part * (1.0 - identity) + diagonal_part[:, :, None] * identity


def draw_coarse_inverse(key, part):
    first, second = jax.random.split(key)
    count = NAGG * BANDS
    weight = 1.0 / math.sqrt(AGG_CELLS)
    off_part = 0.05 * jnp.clip(jax.random.normal(first, (count, count), jnp.float32), -4.0, 4.0)
    diagonal_part = jnp.exp(jax.random.uniform(second, (count,), jnp.float32, math.log(0.5), math.log(2.0)))
    identity = jnp.eye(count, dtype=jnp.float32)
    return weight * (off_part * (1.0 - identity) + diagonal_part[:, None] * identity)


def with_ends(array, own_key, smallest, top_value):
    place = [jax.random.randint(jax.random.fold_in(own_key, axis), (), 0, length) for axis, length in enumerate(array.shape)]
    widest = array.shape.index(max(array.shape))
    beside = place[:widest] + [(place[widest] + 1) % array.shape[widest]] + place[widest + 1:]
    return array.at[tuple(place)].set(smallest).at[tuple(beside)].set(top_value)


def setup_inputs(seed: int = 0) -> dict:
    keys = jax.random.split(jax.random.key(seed), 7)
    return {
        "right_hand": draw_right_hand(jax.random.fold_in(keys[6], 71), 0),
        "region_labels": with_ends(jax.random.randint(keys[1], (NX, NY * NZ), 0, REGIONS), jax.random.fold_in(keys[1], 1), 0, REGIONS - 1).astype(jnp.int32),
        "potential_table": jnp.clip(jnp.exp(jax.random.uniform(keys[2], (REGIONS, BANDS), jnp.float32, math.log(0.5), math.log(3.0))), 0.5, 3.0),
        "coupling": draw_coupling(jax.random.fold_in(keys[6], 71), 0),
        "aggregate_map": with_ends(jax.random.randint(keys[4], (NX // 4, (NY // 4) * (NZ // 4)), 0, NAGG), jax.random.fold_in(keys[4], 1), 0, NAGG - 1).astype(jnp.int32),
        "coarse_inverse": draw_coarse_inverse(jax.random.fold_in(keys[6], 71), 0),
    }


HIGHEST = lax.Precision.HIGHEST
OMEGA = 0.7

def couple(matrix, values):
    return jnp.einsum('ab,vbxyz->vaxyz', matrix, values, precision=HIGHEST)

def stencil(padded, values, coupling, potential, depth_index):
    level_scale = 0.25 ** depth_index
    along_x = padded[:, :, 2:, 1:-1, 1:-1] + padded[:, :, :-2, 1:-1, 1:-1]
    along_y = padded[:, :, 1:-1, 2:, 1:-1] + padded[:, :, 1:-1, :-2, 1:-1]
    along_z = padded[:, :, 1:-1, 1:-1, 2:] + padded[:, :, 1:-1, 1:-1, :-2]
    centre = 2.0 * level_scale * (coupling[0] + coupling[1] + coupling[2])
    result = couple(centre, values) - couple(level_scale * coupling[0], along_x)
    result = result - couple(level_scale * coupling[1], along_y) - couple(level_scale * coupling[2], along_z)
    return result + potential[None] * values

def restrict(values):
    leading = values.shape[:-3]
    size_x, size_y, size_z = values.shape[-3:]
    grouped = values.reshape(leading + (size_x // 2, 2, size_y // 2, 2, size_z // 2, 2))
    offset = len(leading)
    return lax.optimization_barrier(jnp.mean(grouped, axis=(offset + 1, offset + 3, offset + 5)))

def prolong(values):
    return jnp.repeat(jnp.repeat(jnp.repeat(values, 2, axis=2), 2, axis=3), 2, axis=4)

def inverse_diagonal(coupling, potential, depth_index):
    level_scale = 0.25 ** depth_index
    centre = 2.0 * level_scale * (coupling[0] + coupling[1] + coupling[2])
    return 1.0 / (jnp.diagonal(centre)[:, None, None, None] + potential)

def vcycle(residual, depth_index, operator, coarsest, inverses):
    correction = OMEGA * inverses[depth_index] * residual
    defect = residual - operator(correction, depth_index)
    if depth_index + 1 < LEVELS:
        correction = correction + prolong(vcycle(restrict(defect), depth_index + 1, operator, coarsest, inverses))
    else:
        correction = correction + coarsest(defect)
    return correction + OMEGA * inverses[depth_index] * (residual - operator(correction, depth_index))

def solve_small(normal_matrix, right_side, count):
    factor = {}
    for i in range(count):
        for k in range(i + 1):
            running = normal_matrix[i][k]
            for m in range(k):
                running = running - factor[i, m] * factor[k, m]
            if i == k:
                factor[i, i] = jnp.sqrt(running)
            else:
                factor[i, k] = running / factor[k, k]
    forward = []
    for i in range(count):
        running = right_side[i]
        for k in range(i):
            running = running - factor[i, k] * forward[k]
        forward.append(running / factor[i, i])
    answer = [None] * count
    for i in reversed(range(count)):
        running = forward[i]
        for k in range(i + 1, count):
            running = running - factor[k, i] * answer[k]
        answer[i] = running / factor[i, i]
    return answer

def inner_product(left, right_side):
    return lax.optimization_barrier(jnp.sum(left * right_side, axis=(1, 2, 3, 4)))

def expand(values):
    return values[:, None, None, None, None]

def least_squares(hessenberg, initial_norm):
    normal_matrix = [[None] * ITERS for i in range(ITERS)]
    for j in range(ITERS):
        for k in range(ITERS):
            running = hessenberg[0][j] * hessenberg[0][k]
            for i in range(1, ITERS + 1):
                running = running + hessenberg[i][j] * hessenberg[i][k]
            normal_matrix[j][k] = running
    right_side = [initial_norm * hessenberg[0][j] for j in range(ITERS)]
    return solve_small(normal_matrix, right_side, ITERS)

def reference(right_hand, region_labels, potential_table, coupling, aggregate_map, coarse_inverse):
    source = right_hand.reshape(VECS, BANDS, NX, NY, NZ)
    cell_labels = region_labels.reshape(NX, NY, NZ)
    potential = jnp.zeros((BANDS, NX, NY, NZ), jnp.float32)
    for r in range(REGIONS):
        potential = potential + jnp.where(cell_labels == r, potential_table[r][:, None, None, None], 0.0)
    potentials = [potential]
    for depth_index in range(1, LEVELS):
        potentials.append(restrict(potentials[-1]))
    inverses = [inverse_diagonal(coupling, potentials[d], d) for d in range(LEVELS)]
    onehot = (aggregate_map.reshape(-1)[:, None] == jnp.arange(NAGG, dtype=jnp.int32)[None, :]).astype(jnp.float32)

    def operator(values, depth_index):
        padded = jnp.pad(values, ((0, 0), (0, 0), (1, 1), (1, 1), (1, 1)))
        return stencil(padded, values, coupling, potentials[depth_index], depth_index)

    def coarsest(defect):
        flattened = defect.reshape(VECS, BANDS, -1)
        partial_value = jnp.einsum('vbc,ca->abv', flattened, onehot, precision=HIGHEST).reshape(NAGG * BANDS, VECS)
        solved = jnp.dot(coarse_inverse, partial_value, precision=HIGHEST).reshape(NAGG, BANDS, VECS)
        return jnp.einsum('ca,abv->vbc', onehot, solved, precision=HIGHEST).reshape(defect.shape)
    initial_norm = jnp.sqrt(inner_product(source, source))
    krylov_basis = [source / expand(initial_norm)]
    zeros_vec = jnp.zeros((VECS,), jnp.float32)
    hessenberg = [[zeros_vec] * ITERS for i in range(ITERS + 1)]
    for j in range(ITERS):
        mapped = operator(vcycle(krylov_basis[j], 0, operator, coarsest, inverses), 0)
        projection = [inner_product(krylov_basis[i], mapped) for i in range(j + 1)]
        for i in range(j + 1):
            mapped = mapped - expand(projection[i]) * krylov_basis[i]
            hessenberg[i][j] = projection[i]
        hessenberg[j + 1][j] = jnp.sqrt(inner_product(mapped, mapped))
        if j + 1 < ITERS:
            krylov_basis.append(mapped / expand(hessenberg[j + 1][j]))
    weights = least_squares(hessenberg, initial_norm)
    combined = expand(weights[0]) * krylov_basis[0]
    for j in range(1, ITERS):
        combined = combined + expand(weights[j]) * krylov_basis[j]
    solution = vcycle(combined, 0, operator, coarsest, inverses)
    return solution.reshape(VECS, BANDS, NX, NY * NZ)
```

```python
import functools
import math

import jax
import jax.numpy as jnp
from jax import lax
from jax.experimental import pallas as pl
from jax.experimental.pallas import tpu as pltpu
from jax.sharding import PartitionSpec as P

NZ = 48
BANDS = 6
VECS = 4
REGIONS = 3
ITERS = 3
NAGG = 64
OMEGA = 0.7

HIGHEST = lax.Precision.HIGHEST
F32 = jnp.float32
BF16 = jnp.bfloat16

TX = 4
TY = 8
YT = 2
ZT = 6
COMBOS = YT * ZT
ZQ = NZ // ZT
GROUP = (TY // YT) * ZQ
TILES = 3
FIELD_ROWS = TILES * BANDS * TX
LABEL_ROWS = TILES * TX
AGG_ROW = FIELD_ROWS + LABEL_ROWS
ROWS = 88
LANES = 128
CELLS = TY * NZ


def source_lane(target):
    combo = target // GROUP
    rest = target % GROUP
    return ((rest // ZQ) * YT + combo // ZT) * NZ + (rest % ZQ) * ZT + combo % ZT


def iota(shape, dim):
    return lax.broadcasted_iota(jnp.int32, shape, dim)


def pack_kernel(groups, right_hbm, labels_hbm, agg_hbm, *rest):
    outs, (stack, right_ref, labels_ref, agg_ref, arrived) = rest[:VECS], rest[VECS:]
    own = lax.axis_index("gx") // groups
    copies = [
        pltpu.make_async_copy(source, target, arrived.at[i])
        for i, (source, target) in enumerate(
            ((right_hbm, right_ref), (labels_hbm, labels_ref), (agg_hbm, agg_ref))
        )
    ]
    for copy in copies:
        copy.start()
    permute = (iota((CELLS, CELLS), 0) == source_lane(iota((1, CELLS), 1))).astype(F32)
    count = BANDS * TX
    for copy in copies:
        copy.wait()
    for k in range(VECS):
        for b in range(BANDS):
            stack[pl.ds(k * count + b * TX, TX), :] = right_ref[own ^ k, b]
    stack[pl.ds(VECS * count, TX), :] = labels_ref[...].astype(F32)
    stack[pl.ds(VECS * count + TX, TX), :] = jnp.zeros((TX, CELLS), F32)
    moved = jnp.dot(stack[...], permute, precision=HIGHEST, preferred_element_type=F32)
    lane = iota((1, LANES), 1)
    inner = lane % GROUP
    wanted = (inner // (2 * ZQ)) * (NZ // 4) + 3 * ((inner % ZQ) // 2) + lane // GROUP
    wanted = jnp.where(lane < 3 * GROUP, wanted, -1)
    cells = agg_ref.shape[1]
    pick = (iota((cells, LANES), 0) == wanted).astype(F32)
    agg = jnp.dot(
        jnp.broadcast_to(agg_ref[...].astype(F32), (8, cells)),
        pick,
        precision=HIGHEST,
        preferred_element_type=F32,
    )
    for k in range(VECS):
        for t in range(TILES):
            tile = slice(t * LANES, (t + 1) * LANES)
            outs[k][pl.ds(t * count, count), :] = moved[k * count : (k + 1) * count, tile]
            outs[k][pl.ds(FIELD_ROWS + t * TX, TX), :] = moved[
                VECS * count : VECS * count + TX, tile
            ]
        outs[k][pl.ds(AGG_ROW, ROWS - AGG_ROW), :] = agg[: ROWS - AGG_ROW]


def unpack_kernel(groups, *refs):
    ins, out_ref, stack = refs[:VECS], refs[VECS], refs[VECS + 1]
    own = lax.axis_index("gx") // groups
    count = BANDS * TX
    permute = (iota((CELLS, CELLS), 1) == source_lane(iota((CELLS, 1), 0))).astype(F32)
    for k in range(VECS):
        for t in range(TILES):
            stack[pl.ds(k * count, count), t * LANES : (t + 1) * LANES] = ins[k][
                pl.ds(t * count, count), :
            ]
    moved = jnp.dot(stack[...], permute, precision=HIGHEST, preferred_element_type=F32)
    for k in range(VECS):
        for b in range(BANDS):
            first = k * count + b * TX
            out_ref[own ^ k, b] = moved[first : first + TX]


def order_kernel(source_ref, out_ref):
    size = NAGG * BANDS
    column = iota((1, size), 1)
    inputs = (iota((size, size), 0) == (column % NAGG) * BANDS + column // NAGG).astype(F32)
    wide = iota((1, BANDS * LANES), 1)
    place = wide % LANES
    wanted = jnp.where(place < NAGG, place * BANDS + wide // LANES, -1)
    outputs = (iota((size, BANDS * LANES), 0) == wanted).astype(F32)
    turned = jnp.dot(source_ref[...], inputs, precision=HIGHEST, preferred_element_type=F32)
    out_ref[...] = lax.dot_general(
        turned,
        outputs,
        (((0,), (0,)), ((), ())),
        precision=HIGHEST,
        preferred_element_type=F32,
    ).reshape(BANDS, NAGG, BANDS * LANES)


def solve_kernel(size_x, size_y, steps, *refs):
    count = len(steps) + 1
    pieces, (coef, table, inverse_ref) = refs[:count], refs[count : count + 3]
    refs = refs[count - 1 :]
    outs = refs[4 : 4 + VECS]
    (
        scratch, basis, ext_a, ext_b, pots, winv, sums, labels, aggs, onehot, pots_1, winv_1,
        pots_2, winv_2, res_1, cor_1, res_2, cor_2, cells_2, kept, hess, scale, answer, arrived,
    ) = refs[4 + VECS :]
    groups = size_x // VECS
    lanes = size_y * GROUP
    plane = (size_x, lanes)
    halves = lanes // LANES
    my_x = lax.axis_index("gx")
    my_y = lax.axis_index("gy")
    own = my_x // groups
    my_g = my_x % groups

    sub = iota(plane, 0)
    lane = iota(plane, 1)
    first_x, last_x = sub == 0, sub == size_x - 1
    first_y, last_y = lane < ZQ, lane >= lanes - ZQ
    first_z, last_z = lane % ZQ == 0, lane % ZQ == ZQ - 1

    def shifted(value, amount, axis, mask):
        moved = pltpu.roll(value, amount % value.shape[axis], axis)
        return jnp.where(mask, 0.0, moved)

    def coupling(direction, a, b):
        return coef[direction, a, b]

    def centre(band):
        return 2.0 * (coupling(0, band, band) + coupling(1, band, band) + coupling(2, band, band))

    copies = []
    for i, piece in enumerate(pieces):
        first = (1 << i) >> 1
        for place in range(first, 1 << i):
            mask_g = mask_y = 0
            for n, (axis, bit) in enumerate(steps):
                here = ((place >> n) & 1) << bit
                mask_g, mask_y = (mask_g | here, mask_y) if axis == "gx" else (mask_g, mask_y | here)
            for k in range(VECS):
                target = scratch.at[:, my_y ^ mask_y, (own ^ k) * groups + (my_g ^ mask_g), :]
                source = piece.at[(place - first) * VECS + k]
                copies.append(pltpu.make_async_copy(source, target, arrived.at[len(copies)]))
    for copy in copies:
        copy.start()
    for copy in copies:
        copy.wait()

    one_lane = iota((size_x, LANES), 1)
    low_64, low_32 = one_lane < 64, one_lane % 64 < 32

    def regroup(row):
        result = []
        for h in range(halves):
            g = [scratch[row, 4 * h + i] for i in range(4)]
            for i in (0, 1):
                low, high = g[i], g[i + 2]
                g[i] = jnp.where(low_64, low, pltpu.roll(high, 64, 1))
                g[i + 2] = jnp.where(low_64, pltpu.roll(low, 64, 1), high)
            for i in (0, 2):
                low, high = g[i], g[i + 1]
                g[i] = jnp.where(low_32, low, pltpu.roll(high, 32, 1))
                g[i + 1] = jnp.where(low_32, pltpu.roll(low, 96, 1), high)
            result.append(g)
        return [
            result[0][c] if halves == 1 else jnp.concatenate([r[c] for r in result], axis=1)
            for c in range(4)
        ]

    def load_field(x, total):
        for t in range(TILES):
            for b in range(BANDS):
                for c, value in enumerate(regroup(t * BANDS * TX + b * TX + x)):
                    basis[0, x, t * 4 + c, b] = value
                    total = total + value * value
            for c, value in enumerate(regroup(FIELD_ROWS + t * TX + x)):
                labels[x, t * 4 + c] = value
        return total

    total = lax.fori_loop(0, TX, load_field, jnp.zeros(plane, F32))
    for k, value in enumerate(regroup(AGG_ROW)[:3]):
        aggs[k] = value

    def total_of(value):
        return jnp.broadcast_to(jnp.sum(value, keepdims=True), plane)

    beta = jnp.sqrt(total_of(total))
    scale[...] = 1.0 / beta
    for i in range((ITERS + 1) * ITERS):
        hess[i] = jnp.zeros(plane, F32)

    def fill(x, carry):
        for b in range(BANDS):
            diagonal = centre(b)
            for zt in range(ZT):
                for yt in range(YT):
                    label = labels[x, yt * ZT + zt]
                    value = jnp.zeros(plane, F32)
                    for r in range(REGIONS):
                        value = jnp.where(label == float(r), table[r, b], value)
                    pots[x, yt * ZT + zt, b] = value
                    winv[x, yt * ZT + zt, b] = OMEGA * (1.0 / (diagonal + value))
                    if zt % 2 == 0 and yt == 0:
                        four = value
                    else:
                        four = four + value
                if zt % 2 == 1:
                    sums[x, zt // 2, b] = four
        return carry

    lax.fori_loop(0, TX, fill, 0)

    even_z = lane % 2 == 0
    even_y = (lane // ZQ) % 2 == 0

    def restrict_2(q):
        near, far = q[0] + q[1], q[1] + q[2]
        p = [
            jnp.where(even_z, near, pltpu.roll(near, 1, 1)),
            jnp.where(even_z, q[2], q[0])
            + jnp.where(even_z, pltpu.roll(q[0], lanes - 1, 1), pltpu.roll(q[2], 1, 1)),
            jnp.where(even_z, pltpu.roll(far, lanes - 1, 1), far),
        ]
        return [
            0.125
            * (v + jnp.where(even_y, pltpu.roll(v, lanes - ZQ, 1), pltpu.roll(v, ZQ, 1)))
            for v in p
        ]

    for b in range(BANDS):
        q = []
        for z in range(3):
            pair = []
            for x in range(2):
                value = 0.125 * (sums[2 * x, z, b] + sums[2 * x + 1, z, b])
                pots_1[x, z, b] = value
                winv_1[x, z, b] = OMEGA * (1.0 / (0.25 * centre(b) + value))
                pair.append(value)
            q.append(pair[0] + pair[1])
        for k, value in enumerate(restrict_2(q)):
            pots_2[k, b] = value
            winv_2[k, b] = OMEGA * (1.0 / (0.0625 * centre(b) + value))

    for k in range(3):
        for h in range(halves):
            for x in range(size_x):
                n = (k * halves + h) * size_x + x
                row = aggs[k, x : x + 1, h * LANES : (h + 1) * LANES]
                onehot[:, n * LANES : (n + 1) * LANES] = (
                    (row == iota((NAGG, LANES), 0).astype(F32)).astype(F32).astype(BF16)
                )

    def ghosts(ext):
        for c in range(COMBOS):
            for b in range(BANDS):
                ext[TX + 1, c, b] = shifted(ext[1, c, b], -1, 0, last_x)
                ext[0, c, b] = shifted(ext[TX, c, b], 1, 0, first_x)

    def combine(neighbours, count):
        acc = None
        for b in range(BANDS):
            differences = neighbours(b)
            new = []
            for a in range(BANDS):
                c = [coupling(d, a, b) for d in range(3)]
                row = []
                for n in range(count):
                    value = c[0] * differences[0][n]
                    value = value + c[1] * differences[1][n]
                    value = value + c[2] * differences[2][n]
                    row.append(value if acc is None else acc[a][n] + value)
                new.append(row)
            acc = new
        return acc

    def operator_0(ext, x, finish):
        for pair in range(ZT // 2):
            cells = [(yt, 2 * pair + i) for i in range(2) for yt in range(YT)]

            def neighbours(b):
                def at(dx, yt, zt):
                    return ext[x + 1 + dx, yt * ZT + zt, b]

                mid = {cell: at(0, *cell) for cell in cells}
                along = [[], [], []]
                for yt, zt in cells:
                    twice = mid[yt, zt] + mid[yt, zt]
                    along[0].append(twice - (at(1, yt, zt) + at(-1, yt, zt)))
                    partner = mid[1 - yt, zt]
                    if yt == 0:
                        outer = shifted(partner, ZQ, 1, first_y)
                    else:
                        outer = shifted(partner, -ZQ, 1, last_y)
                    along[1].append(twice - (partner + outer))
                    if zt % 2 == 0:
                        inside = mid[yt, zt + 1]
                        if zt == 0:
                            outer = shifted(at(0, yt, ZT - 1), 1, 1, first_z)
                        else:
                            outer = at(0, yt, zt - 1)
                    else:
                        inside = mid[yt, zt - 1]
                        if zt == ZT - 1:
                            outer = shifted(at(0, yt, 0), -1, 1, last_z)
                        else:
                            outer = at(0, yt, zt + 1)
                    along[2].append(twice - (inside + outer))
                return along

            acc = combine(neighbours, len(cells))
            values = [
                [
                    acc[b][n] + pots[x, yt * ZT + zt, b] * ext[x + 1, yt * ZT + zt, b]
                    for n, (yt, zt) in enumerate(cells)
                ]
                for b in range(BANDS)
            ]
            finish(pair, cells, values)

    def operator_1(src, finish):
        for x in range(2):

            def neighbours(b):
                along = [[], [], []]
                mid = [src[x, z, b] for z in range(3)]
                for z in range(3):
                    twice = mid[z] + mid[z]
                    partner = src[1 - x, z, b]
                    if x == 0:
                        outer = shifted(partner, 1, 0, first_x)
                    else:
                        outer = shifted(partner, -1, 0, last_x)
                    along[0].append(twice - (partner + outer))
                    along[1].append(
                        twice
                        - (shifted(mid[z], ZQ, 1, first_y) + shifted(mid[z], -ZQ, 1, last_y))
                    )
                    below = mid[z - 1] if z > 0 else shifted(mid[2], 1, 1, first_z)
                    above = mid[z + 1] if z < 2 else shifted(mid[0], -1, 1, last_z)
                    along[2].append(twice - (below + above))
                return along

            acc = combine(neighbours, 3)
            finish(
                x,
                [
                    [0.25 * acc[b][z] + pots_1[x, z, b] * src[x, z, b] for z in range(3)]
                    for b in range(BANDS)
                ],
            )

    first_y2, last_y2 = lane < 2 * ZQ, lane >= lanes - 2 * ZQ
    first_z2, last_z2 = lane % ZQ < 2, lane % ZQ >= ZQ - 2

    def operator_2(src):
        def neighbours(b):
            along = [[], [], []]
            mid = [src[z, b] for z in range(3)]
            for z in range(3):
                twice = mid[z] + mid[z]
                along[0].append(
                    twice - (shifted(mid[z], 1, 0, first_x) + shifted(mid[z], -1, 0, last_x))
                )
                along[1].append(
                    twice
                    - (
                        shifted(mid[z], 2 * ZQ, 1, first_y2)
                        + shifted(mid[z], -2 * ZQ, 1, last_y2)
                    )
                )
                below = mid[z - 1] if z > 0 else shifted(mid[2], 2, 1, first_z2)
                above = mid[z + 1] if z < 2 else shifted(mid[0], -2, 1, last_z2)
                along[2].append(twice - (below + above))
            return along

        acc = combine(neighbours, 3)
        return [
            [0.0625 * acc[b][z] + pots_2[z, b] * src[z, b] for z in range(3)] for b in range(BANDS)
        ]

    def split(value):
        high = value.astype(BF16)
        left = value - high.astype(F32)
        middle = left.astype(BF16)
        low = (left - middle.astype(F32)).astype(BF16)
        return jnp.concatenate([high, middle, low], axis=0)

    single = even_y & even_z
    count_2 = 3 * halves * size_x

    def coarse(defect):
        for z in range(3):
            for b in range(8):
                if b < BANDS:
                    value = jnp.where(single, defect[b][z], 0.0)
                else:
                    value = jnp.zeros(plane, F32)
                for h in range(halves):
                    n = (z * halves + h) * size_x
                    cells_2[pl.ds(n * 8 + b, size_x, stride=8), :] = value[
                        :, h * LANES : (h + 1) * LANES
                    ]
        wide = jnp.concatenate(
            [cells_2[pl.ds(n * 8, 8), :] for n in range(count_2)], axis=1
        )
        partial = lax.dot_general(
            onehot[...],
            split(wide),
            (((1,), (1,)), ((), ())),
            preferred_element_type=F32,
        )
        partial = partial[:, :8] + partial[:, 8:16] + partial[:, 16:24]
        acc = [jnp.zeros((8, LANES), F32)] * BANDS
        for b in range(BANDS):
            column = jnp.broadcast_to(partial[:, b : b + 1], (NAGG, LANES))
            for i in range(NAGG // 8):
                for a in range(BANDS):
                    acc[a] = (
                        acc[a]
                        + inverse_ref[b, pl.ds(i * 8, 8), a * LANES : (a + 1) * LANES]
                        * column[i * 8 : (i + 1) * 8]
                    )
        band = iota((8, LANES), 0)
        solved = jnp.zeros((8, LANES), F32)
        for a in range(BANDS):
            solved = jnp.where(band == a, jnp.sum(acc[a], axis=0, keepdims=True), solved)
        spread_out = jnp.dot(
            split(solved[:, :NAGG]), onehot[...], preferred_element_type=F32
        )
        spread_out = spread_out[:8] + spread_out[8:16] + spread_out[16:24]
        for n in range(count_2):
            cells_2[pl.ds(n * 8, 8), :] = spread_out[:, n * LANES : (n + 1) * LANES]

        def correction(b, z):
            parts = [
                cells_2[pl.ds(((z * halves + h) * size_x) * 8 + b, size_x, stride=8), :]
                for h in range(halves)
            ]
            return parts[0] if halves == 1 else jnp.concatenate(parts, axis=1)

        return correction

    def iteration(j, carry):
        factor = scale[...]

        def smooth(x, c_):
            for c in range(COMBOS):
                for b in range(BANDS):
                    value = basis[j, x, c, b] * factor
                    basis[j, x, c, b] = value
                    ext_a[x + 1, c, b] = winv[x, c, b] * value
            return c_

        lax.fori_loop(0, TX, smooth, 0)
        ghosts(ext_a)

        def down(x, c_):
            def finish(pair, cells, values):
                for b in range(BANDS):
                    defects = [
                        basis[j, x, yt * ZT + zt, b] - values[b][n]
                        for n, (yt, zt) in enumerate(cells)
                    ]
                    sums[x, pair, b] = (defects[0] + defects[1]) + (defects[2] + defects[3])

            operator_0(ext_a, x, finish)
            return c_

        lax.fori_loop(0, TX, down, 0)

        for x in range(2):
            for z in range(3):
                for b in range(BANDS):
                    value = 0.125 * (sums[2 * x, z, b] + sums[2 * x + 1, z, b])
                    res_1[x, z, b] = value
                    cor_1[x, z, b] = winv_1[x, z, b] * value

        held = {}

        def defect_1(x, values):
            for b in range(BANDS):
                for z in range(3):
                    value = res_1[x, z, b] - values[b][z]
                    if x == 0:
                        sums[0, z, b] = value
                    else:
                        sums[0, z, b] = sums[0, z, b] + value

        operator_1(cor_1, defect_1)
        for b in range(BANDS):
            for z, value in enumerate(restrict_2([sums[0, z, b] for z in range(3)])):
                res_2[z, b] = value
                cor_2[z, b] = winv_2[z, b] * value
        values = operator_2(cor_2)
        correction = coarse(
            [[res_2[z, b] - values[b][z] for z in range(3)] for b in range(BANDS)]
        )
        for b in range(BANDS):
            for z in range(3):
                cor_2[z, b] = cor_2[z, b] + correction(b, z)
        values = operator_2(cor_2)
        for b in range(BANDS):
            e = [
                cor_2[z, b] + winv_2[z, b] * (res_2[z, b] - values[b][z]) for z in range(3)
            ]
            fine = [
                jnp.where(even_z, e[0], e[1]),
                jnp.where(even_z, e[0], e[2]),
                jnp.where(even_z, e[1], e[2]),
            ]
            for x in range(2):
                for z in range(3):
                    cor_1[x, z, b] = cor_1[x, z, b] + fine[z]

        def post_1(x, values):
            for b in range(BANDS):
                for z in range(3):
                    sums[x, z, b] = cor_1[x, z, b] + winv_1[x, z, b] * (
                        res_1[x, z, b] - values[b][z]
                    )

        operator_1(cor_1, post_1)

        def prolong(x, c_):
            for c in range(COMBOS):
                for b in range(BANDS):
                    ext_a[x + 1, c, b] = ext_a[x + 1, c, b] + sums[x // 2, (c % ZT) // 2, b]
            return c_

        lax.fori_loop(0, TX, prolong, 0)
        ghosts(ext_a)

        def up(x, c_):
            def finish(pair, cells, values):
                for b in range(BANDS):
                    for n, (yt, zt) in enumerate(cells):
                        c = yt * ZT + zt
                        ext_b[x + 1, c, b] = ext_a[x + 1, c, b] + winv[x, c, b] * (
                            basis[j, x, c, b] - values[b][n]
                        )

            operator_0(ext_a, x, finish)
            return c_

        lax.fori_loop(0, TX, up, 0)
        ghosts(ext_b)

        def apply(x, c_):
            def finish(pair, cells, values):
                for b in range(BANDS):
                    for n, (yt, zt) in enumerate(cells):
                        basis[j + 1, x, yt * ZT + zt, b] = values[b][n]

            operator_0(ext_b, x, finish)
            quarter = one_lane // GROUP
            for b in range(BANDS):
                for t in range(TILES):
                    merged = None
                    for i in range(4):
                        moved = pltpu.roll(
                            ext_b[x + 1, t * 4 + i, b], (GROUP * i + lanes - GROUP * my_y) % lanes, 1
                        )[:, :LANES]
                        merged = moved if i == 0 else jnp.where(quarter == i, moved, merged)
                    kept[j, x, b * TILES + t] = merged
            return c_

        lax.fori_loop(0, TX, apply, 0)

        def project(i, c_):
            def body(x, parts):
                parts = list(parts)
                for c in range(COMBOS):
                    for b in range(BANDS):
                        n = (c * BANDS + b) % 4
                        parts[n] = parts[n] + basis[i, x, c, b] * basis[j + 1, x, c, b]
                return tuple(parts)

            parts = lax.fori_loop(0, TX, body, (jnp.zeros(plane, F32),) * 4)
            hess[i * ITERS + j] = total_of((parts[0] + parts[1]) + (parts[2] + parts[3]))
            return c_

        lax.fori_loop(0, j + 1, project, 0)

        def subtract(i, c_):
            weight = hess[i * ITERS + j]

            def body(x, parts):
                parts = list(parts)
                for c in range(COMBOS):
                    for b in range(BANDS):
                        n = (c * BANDS + b) % 4
                        value = basis[j + 1, x, c, b] - weight * basis[i, x, c, b]
                        basis[j + 1, x, c, b] = value
                        parts[n] = parts[n] + value * value
                return tuple(parts)

            parts = lax.fori_loop(0, TX, body, (jnp.zeros(plane, F32),) * 4)
            return (parts[0] + parts[1]) + (parts[2] + parts[3])

        total = lax.fori_loop(0, j + 1, subtract, jnp.zeros(plane, F32))
        norm = jnp.sqrt(total_of(total))
        hess[(j + 1) * ITERS + j] = norm
        scale[...] = 1.0 / norm
        return carry

    lax.fori_loop(0, ITERS, iteration, 0)

    h = [[hess[i * ITERS + j][:, :LANES] for j in range(ITERS)] for i in range(ITERS + 1)]
    normal = [
        [sum(h[i][j] * h[i][k] for i in range(ITERS + 1)) for k in range(ITERS)]
        for j in range(ITERS)
    ]
    first = beta[:, :LANES]
    weights = solve_small(normal, [first * h[0][j] for j in range(ITERS)], ITERS)

    for x in range(TX):
        for b in range(BANDS):
            for t in range(TILES):
                value = weights[0] * kept[0, x, b * TILES + t]
                for j in range(1, ITERS):
                    value = value + weights[j] * kept[j, x, b * TILES + t]
                value = pltpu.roll(value, (size_x - my_g) % size_x, 0)
                row = t * BANDS * TX + b * TX + x
                for z in range(VECS):
                    answer[z, row : row + 1, :] = value[z * groups : z * groups + 1]
    for k in range(VECS):
        outs[k][...] = answer[own ^ k]


def solve_small(normal_matrix, right_side, count):
    factor = {}
    for i in range(count):
        for k in range(i + 1):
            running = normal_matrix[i][k]
            for m in range(k):
                running = running - factor[i, m] * factor[k, m]
            if i == k:
                factor[i, i] = jnp.sqrt(running)
            else:
                factor[i, k] = running / factor[k, k]
    forward = []
    for i in range(count):
        running = right_side[i]
        for k in range(i):
            running = running - factor[i, k] * forward[k]
        forward.append(running / factor[i, i])
    answer = [None] * count
    for i in reversed(range(count)):
        running = forward[i]
        for k in range(i + 1, count):
            running = running - factor[k, i] * answer[k]
        answer[i] = running / factor[i, i]
    return answer


VMEM_SPEC = pl.BlockSpec(memory_space=pltpu.VMEM)
ANY_SPEC = pl.BlockSpec(memory_space=pl.ANY)
SMEM_SPEC = pl.BlockSpec(memory_space=pltpu.SMEM)


def bits(count):
    return count.bit_length() - 1


def shards(
    size_x, size_y, right_hand, region_labels, potential_table, coupling, aggregate_map,
    coarse_inverse,
):
    groups = size_x // VECS
    devices = size_x * size_y
    names = ("gx", "gy")
    stride = groups * size_y

    def exchanged(value, mask):
        return lax.ppermute(value, names, [(i, i ^ mask) for i in range(devices)])

    row_shape = jax.ShapeDtypeStruct((ROWS, LANES), F32)
    count = BANDS * TX
    packed = pl.pallas_call(
        functools.partial(pack_kernel, groups),
        out_shape=[row_shape] * VECS,
        in_specs=[ANY_SPEC] * 3,
        out_specs=[VMEM_SPEC] * VECS,
        scratch_shapes=[
            pltpu.VMEM((VECS * count + 8, CELLS), F32),
            pltpu.VMEM(right_hand.shape, F32),
            pltpu.VMEM(region_labels.shape, jnp.int32),
            pltpu.VMEM(aggregate_map.shape, jnp.int32),
            pltpu.SemaphoreType.DMA((3,)),
        ],
        compiler_params=pltpu.CompilerParams(vmem_limit_bytes=8 * 2**20),
        name="pack",
    )(right_hand, region_labels, aggregate_map)
    parts = [packed[0]] + [exchanged(packed[k], k * stride) for k in range(1, VECS)]
    block = jnp.stack(parts)
    steps = [("gy", i) for i in range(bits(size_y) - 1, 0, -1)]
    steps += [("gx", i) for i in range(bits(groups))]
    steps += [("gy", 0)]
    pieces = [block]
    for axis, bit in steps:
        mask = (1 << bit) * (size_y if axis == "gx" else 1)
        pieces.append(exchanged(jnp.concatenate(pieces, axis=0), mask))

    inverse = pl.pallas_call(
        order_kernel,
        out_shape=jax.ShapeDtypeStruct((BANDS, NAGG, BANDS * LANES), F32),
        in_specs=[VMEM_SPEC],
        out_specs=VMEM_SPEC,
        compiler_params=pltpu.CompilerParams(vmem_limit_bytes=16 * 2**20),
        cost_estimate=pl.CostEstimate(
            flops=6 * (NAGG * BANDS) ** 3, bytes_accessed=2**21, transcendentals=0
        ),
        name="order",
    )(coarse_inverse)

    lanes = size_y * GROUP
    plane = (size_x, lanes)
    count_2 = 3 * (lanes // LANES) * size_x
    vmem = lambda *shape: pltpu.VMEM(shape + plane, F32)
    scratch = [
            pltpu.VMEM((ROWS, size_y, size_x, LANES), F32),
            vmem(ITERS + 1, TX, COMBOS, BANDS),
            vmem(TX + 2, COMBOS, BANDS),
            vmem(TX + 2, COMBOS, BANDS),
            vmem(TX, COMBOS, BANDS),
            vmem(TX, COMBOS, BANDS),
            vmem(TX, 3, BANDS),
            vmem(TX, COMBOS),
            vmem(3),
            pltpu.VMEM((NAGG, count_2 * LANES), BF16),
            vmem(2, 3, BANDS),
            vmem(2, 3, BANDS),
            vmem(3, BANDS),
            vmem(3, BANDS),
            vmem(2, 3, BANDS),
            vmem(2, 3, BANDS),
            vmem(3, BANDS),
            vmem(3, BANDS),
            pltpu.VMEM((count_2 * 8, LANES), F32),
            pltpu.VMEM((ITERS, TX, BANDS * TILES, size_x, LANES), F32),
            vmem((ITERS + 1) * ITERS),
            vmem(),
            pltpu.VMEM((VECS, FIELD_ROWS, LANES), F32),
            pltpu.SemaphoreType.DMA((devices,)),
    ]
    held = sum(math.prod(ref.shape) * 4 for ref in scratch)
    answers = pl.pallas_call(
        functools.partial(solve_kernel, size_x, size_y, tuple(steps)),
        out_shape=[jax.ShapeDtypeStruct((FIELD_ROWS, LANES), F32)] * VECS,
        in_specs=[ANY_SPEC] * len(pieces) + [SMEM_SPEC, SMEM_SPEC, VMEM_SPEC],
        out_specs=[VMEM_SPEC] * VECS,
        scratch_shapes=scratch,
        compiler_params=pltpu.CompilerParams(
            vmem_limit_bytes=min(held + 6 * 2**20, 63 * 2**20)
        ),
        name="solve",
    )(*pieces, coupling, potential_table, inverse)
    received = [answers[0]] + [exchanged(answers[k], k * stride) for k in range(1, VECS)]
    return pl.pallas_call(
        functools.partial(unpack_kernel, groups),
        out_shape=jax.ShapeDtypeStruct(right_hand.shape, F32),
        in_specs=[VMEM_SPEC] * VECS,
        out_specs=VMEM_SPEC,
        scratch_shapes=[pltpu.VMEM((VECS * count, CELLS), F32)],
        compiler_params=pltpu.CompilerParams(vmem_limit_bytes=8 * 2**20),
        name="unpack",
    )(*received)


def solution(mesh):
    return jax.shard_map(
        functools.partial(shards, mesh.shape["gx"], mesh.shape["gy"]),
        mesh=mesh,
        in_specs=(P(None, None, "gx", "gy"), P("gx", "gy"), P(), P(), P("gx", "gy"), P()),
        out_specs=P(None, None, "gx", "gy"),
        check_vma=False,
    )
```

```python
import functools
import math

import jax
import jax.numpy as jnp
from jax import lax
from jax.experimental import pallas as pl
from jax.experimental.pallas import tpu as pltpu
from jax.sharding import PartitionSpec as P

NZ = 48
BANDS = 6
VECS = 4
REGIONS = 3
ITERS = 3
NAGG = 64
OMEGA = 0.7

HIGHEST = lax.Precision.HIGHEST
F32 = jnp.float32
BF16 = jnp.bfloat16

TX = 4
TY = 8
YT = 2
ZT = 6
COMBOS = YT * ZT
ZQ = NZ // ZT
GROUP = (TY // YT) * ZQ
TILES = 3
FIELD_ROWS = TILES * BANDS * TX
LABEL_ROWS = TILES * TX
AGG_ROW = FIELD_ROWS + LABEL_ROWS
ROWS = 88
LANES = 128
CELLS = TY * NZ


def source_lane(target):
    combo = target // GROUP
    rest = target % GROUP
    return ((rest // ZQ) * YT + combo // ZT) * NZ + (rest % ZQ) * ZT + combo % ZT


def iota(shape, dim):
    return lax.broadcasted_iota(jnp.int32, shape, dim)


def pack_kernel(groups, right_hbm, labels_hbm, agg_hbm, *rest):
    outs, (stack, right_ref, labels_ref, agg_ref, arrived) = rest[:VECS], rest[VECS:]
    own = lax.axis_index("gx") // groups
    copies = [
        pltpu.make_async_copy(source, target, arrived.at[i])
        for i, (source, target) in enumerate(
            ((right_hbm, right_ref), (labels_hbm, labels_ref), (agg_hbm, agg_ref))
        )
    ]
    for copy in copies:
        copy.start()
    permute = (iota((CELLS, CELLS), 0) == source_lane(iota((1, CELLS), 1))).astype(F32)
    count = BANDS * TX
    for copy in copies:
        copy.wait()
    for k in range(VECS):
        for b in range(BANDS):
            stack[pl.ds(k * count + b * TX, TX), :] = right_ref[own ^ k, b]
    stack[pl.ds(VECS * count, TX), :] = labels_ref[...].astype(F32)
    stack[pl.ds(VECS * count + TX, TX), :] = jnp.zeros((TX, CELLS), F32)
    moved = jnp.dot(stack[...], permute, precision=HIGHEST, preferred_element_type=F32)
    lane = iota((1, LANES), 1)
    inner = lane % GROUP
    wanted = (inner // (2 * ZQ)) * (NZ // 4) + 3 * ((inner % ZQ) // 2) + lane // GROUP
    wanted = jnp.where(lane < 3 * GROUP, wanted, -1)
    cells = agg_ref.shape[1]
    pick = (iota((cells, LANES), 0) == wanted).astype(F32)
    agg = jnp.dot(
        jnp.broadcast_to(agg_ref[...].astype(F32), (8, cells)),
        pick,
        precision=HIGHEST,
        preferred_element_type=F32,
    )
    for k in range(VECS):
        for t in range(TILES):
            tile = slice(t * LANES, (t + 1) * LANES)
            outs[k][pl.ds(t * count, count), :] = moved[k * count : (k + 1) * count, tile]
            outs[k][pl.ds(FIELD_ROWS + t * TX, TX), :] = moved[
                VECS * count : VECS * count + TX, tile
            ]
        outs[k][pl.ds(AGG_ROW, ROWS - AGG_ROW), :] = agg[: ROWS - AGG_ROW]


def unpack_kernel(groups, *refs):
    ins, out_ref, stack = refs[:VECS], refs[VECS], refs[VECS + 1]
    own = lax.axis_index("gx") // groups
    count = BANDS * TX
    permute = (iota((CELLS, CELLS), 1) == source_lane(iota((CELLS, 1), 0))).astype(F32)
    for k in range(VECS):
        for t in range(TILES):
            stack[pl.ds(k * count, count), t * LANES : (t + 1) * LANES] = ins[k][
                pl.ds(t * count, count), :
            ]
    moved = jnp.dot(stack[...], permute, precision=HIGHEST, preferred_element_type=F32)
    for k in range(VECS):
        for b in range(BANDS):
            first = k * count + b * TX
            out_ref[own ^ k, b] = moved[first : first + TX]


def order_kernel(source_ref, out_ref):
    size = NAGG * BANDS
    column = iota((1, size), 1)
    inputs = (iota((size, size), 0) == (column % NAGG) * BANDS + column // NAGG).astype(F32)
    wide = iota((1, BANDS * LANES), 1)
    place = wide % LANES
    wanted = jnp.where(place < NAGG, place * BANDS + wide // LANES, -1)
    outputs = (iota((size, BANDS * LANES), 0) == wanted).astype(F32)
    turned = jnp.dot(source_ref[...], inputs, precision=HIGHEST, preferred_element_type=F32)
    out_ref[...] = lax.dot_general(
        turned,
        outputs,
        (((0,), (0,)), ((), ())),
        precision=HIGHEST,
        preferred_element_type=F32,
    ).reshape(BANDS, NAGG, BANDS * LANES)


def solve_kernel(size_x, size_y, steps, *refs):
    count = len(steps) + 1
    pieces, (coef, table, inverse_ref) = refs[:count], refs[count : count + 3]
    refs = refs[count - 1 :]
    outs = refs[4 : 4 + VECS]
    (
        scratch, basis, fresh, ext, work, pots, winv, sums, labels, aggs, onehot, pots_1, winv_1,
        pots_2, winv_2, sides, res_1, cor_1, res_2, cor_2, cells_2, kept, hess, scale, answer, arrived,
    ) = refs[4 + VECS :]
    groups = size_x // VECS
    lanes = size_y * GROUP
    plane = (size_x, lanes)
    halves = lanes // LANES
    my_x = lax.axis_index("gx")
    my_y = lax.axis_index("gy")
    own = my_x // groups
    my_g = my_x % groups

    sub = iota(plane, 0)
    lane = iota(plane, 1)
    first_x, last_x = sub == 0, sub == size_x - 1
    first_y, last_y = lane < ZQ, lane >= lanes - ZQ
    first_z, last_z = lane % ZQ == 0, lane % ZQ == ZQ - 1

    def shifted(value, amount, axis, mask):
        moved = pltpu.roll(value, amount % value.shape[axis], axis)
        return jnp.where(mask, 0.0, moved)

    def coupling(direction, a, b):
        return coef[direction, a, b]

    def centre(band):
        return 2.0 * (coupling(0, band, band) + coupling(1, band, band) + coupling(2, band, band))

    copies = []
    for i, piece in enumerate(pieces):
        first = (1 << i) >> 1
        for place in range(first, 1 << i):
            mask_g = mask_y = 0
            for n, (axis, bit) in enumerate(steps):
                here = ((place >> n) & 1) << bit
                mask_g, mask_y = (mask_g | here, mask_y) if axis == "gx" else (mask_g, mask_y | here)
            for k in range(VECS):
                target = scratch.at[:, my_y ^ mask_y, (own ^ k) * groups + (my_g ^ mask_g), :]
                source = piece.at[(place - first) * VECS + k]
                copies.append(pltpu.make_async_copy(source, target, arrived.at[len(copies)]))
    for copy in copies:
        copy.start()
    for copy in copies:
        copy.wait()

    one_lane = iota((size_x, LANES), 1)
    low_64, low_32 = one_lane < 64, one_lane % 64 < 32

    def regroup(row):
        result = []
        for h in range(halves):
            g = [scratch[row, 4 * h + i] for i in range(4)]
            for i in (0, 1):
                low, high = g[i], g[i + 2]
                g[i] = jnp.where(low_64, low, pltpu.roll(high, 64, 1))
                g[i + 2] = jnp.where(low_64, pltpu.roll(low, 64, 1), high)
            for i in (0, 2):
                low, high = g[i], g[i + 1]
                g[i] = jnp.where(low_32, low, pltpu.roll(high, 32, 1))
                g[i + 1] = jnp.where(low_32, pltpu.roll(low, 96, 1), high)
            result.append(g)
        return [
            result[0][c] if halves == 1 else jnp.concatenate([r[c] for r in result], axis=1)
            for c in range(4)
        ]

    def load_field(x, total):
        for t in range(TILES):
            for b in range(BANDS):
                for c, value in enumerate(regroup(t * BANDS * TX + b * TX + x)):
                    work[x, t * 4 + c, b] = value
                    for i in range(1, ITERS):
                        basis[i, x, t * 4 + c, b] = jnp.zeros(plane, F32)
                    total = total + value * value
            for c, value in enumerate(regroup(FIELD_ROWS + t * TX + x)):
                labels[x, t * 4 + c] = value
        return total

    total = lax.fori_loop(0, TX, load_field, jnp.zeros(plane, F32))
    for k, value in enumerate(regroup(AGG_ROW)[:3]):
        aggs[k] = value

    def total_of(value):
        return jnp.broadcast_to(jnp.sum(value, keepdims=True), plane)

    beta = jnp.sqrt(total_of(total))
    scale[...] = 1.0 / beta
    for i in range((ITERS + 1) * ITERS):
        hess[i] = jnp.zeros(plane, F32)

    def fill(x, carry):
        for b in range(BANDS):
            diagonal = centre(b)
            for zt in range(ZT):
                for yt in range(YT):
                    label = labels[x, yt * ZT + zt]
                    value = jnp.zeros(plane, F32)
                    for r in range(REGIONS):
                        value = jnp.where(label == float(r), table[r, b], value)
                    pots[x, yt * ZT + zt, b] = value
                    winv[x, yt * ZT + zt, b] = OMEGA * (1.0 / (diagonal + value))
                    if zt % 2 == 0 and yt == 0:
                        four = value
                    else:
                        four = four + value
                if zt % 2 == 1:
                    sums[x, zt // 2, b] = four
        return carry

    lax.fori_loop(0, TX, fill, 0)

    even_z = lane % 2 == 0
    even_y = (lane // ZQ) % 2 == 0

    def restrict_2(q):
        near, far = q[0] + q[1], q[1] + q[2]
        p = [
            jnp.where(even_z, near, pltpu.roll(near, 1, 1)),
            jnp.where(even_z, q[2], q[0])
            + jnp.where(even_z, pltpu.roll(q[0], lanes - 1, 1), pltpu.roll(q[2], 1, 1)),
            jnp.where(even_z, pltpu.roll(far, lanes - 1, 1), far),
        ]
        return [
            0.125
            * (v + jnp.where(even_y, pltpu.roll(v, lanes - ZQ, 1), pltpu.roll(v, ZQ, 1)))
            for v in p
        ]

    for b in range(BANDS):
        q = []
        for z in range(3):
            pair = []
            for x in range(2):
                value = 0.125 * (sums[2 * x, z, b] + sums[2 * x + 1, z, b])
                pots_1[x, z, b] = value
                winv_1[x, z, b] = OMEGA * (1.0 / (0.25 * centre(b) + value))
                pair.append(value)
            q.append(pair[0] + pair[1])
        for k, value in enumerate(restrict_2(q)):
            pots_2[k, b] = value
            winv_2[k, b] = OMEGA * (1.0 / (0.0625 * centre(b) + value))

    for k in range(3):
        for h in range(halves):
            for x in range(size_x):
                n = (k * halves + h) * size_x + x
                row = aggs[k, x : x + 1, h * LANES : (h + 1) * LANES]
                onehot[:, n * LANES : (n + 1) * LANES] = (
                    (row == iota((NAGG, LANES), 0).astype(F32)).astype(F32).astype(BF16)
                )

    def ghosts():
        for c in range(COMBOS):
            for b in range(BANDS):
                ext[TX + 1, c, b] = shifted(ext[1, c, b], -1, 0, last_x)
                ext[0, c, b] = shifted(ext[TX, c, b], 1, 0, first_x)

    def combine(neighbours, count):
        acc = None
        for b in range(BANDS):
            differences = neighbours(b)
            new = []
            for a in range(BANDS):
                c = [coupling(d, a, b) for d in range(3)]
                row = []
                for n in range(count):
                    value = c[0] * differences[0][n]
                    value = value + c[1] * differences[1][n]
                    value = value + c[2] * differences[2][n]
                    row.append(value if acc is None else acc[a][n] + value)
                new.append(row)
            acc = new
        return acc

    def operator_0(x, finish):
        for pair in range(ZT // 2):
            cells = [(yt, 2 * pair + i) for i in range(2) for yt in range(YT)]

            def neighbours(b):
                def at(dx, yt, zt):
                    return ext[x + 1 + dx, yt * ZT + zt, b]

                mid = {cell: at(0, *cell) for cell in cells}
                along = [[], [], []]
                for yt, zt in cells:
                    twice = mid[yt, zt] + mid[yt, zt]
                    along[0].append(twice - (at(1, yt, zt) + at(-1, yt, zt)))
                    partner = mid[1 - yt, zt]
                    if yt == 0:
                        outer = shifted(partner, ZQ, 1, first_y)
                    else:
                        outer = shifted(partner, -ZQ, 1, last_y)
                    along[1].append(twice - (partner + outer))
                    if zt % 2 == 0:
                        inside = mid[yt, zt + 1]
                        if zt == 0:
                            outer = shifted(at(0, yt, ZT - 1), 1, 1, first_z)
                        else:
                            outer = at(0, yt, zt - 1)
                    else:
                        inside = mid[yt, zt - 1]
                        if zt == ZT - 1:
                            outer = shifted(at(0, yt, 0), -1, 1, last_z)
                        else:
                            outer = at(0, yt, zt + 1)
                    along[2].append(twice - (inside + outer))
                return along

            acc = combine(neighbours, len(cells))
            values = [
                [
                    acc[b][n] + pots[x, yt * ZT + zt, b] * ext[x + 1, yt * ZT + zt, b]
                    for n, (yt, zt) in enumerate(cells)
                ]
                for b in range(BANDS)
            ]
            finish(pair, cells, values)

    def operator_1(src, finish):
        for x in range(2):

            def neighbours(b):
                along = [[], [], []]
                mid = [src[x, z, b] for z in range(3)]
                for z in range(3):
                    twice = mid[z] + mid[z]
                    partner = src[1 - x, z, b]
                    if x == 0:
                        outer = shifted(partner, 1, 0, first_x)
                    else:
                        outer = shifted(partner, -1, 0, last_x)
                    along[0].append(twice - (partner + outer))
                    along[1].append(
                        twice
                        - (shifted(mid[z], ZQ, 1, first_y) + shifted(mid[z], -ZQ, 1, last_y))
                    )
                    below = mid[z - 1] if z > 0 else shifted(mid[2], 1, 1, first_z)
                    above = mid[z + 1] if z < 2 else shifted(mid[0], -1, 1, last_z)
                    along[2].append(twice - (below + above))
                return along

            acc = combine(neighbours, 3)
            finish(
                x,
                [
                    [0.25 * acc[b][z] + pots_1[x, z, b] * src[x, z, b] for z in range(3)]
                    for b in range(BANDS)
                ],
            )

    first_y2, last_y2 = lane < 2 * ZQ, lane >= lanes - 2 * ZQ
    first_z2, last_z2 = lane % ZQ < 2, lane % ZQ >= ZQ - 2

    def operator_2(src):
        def neighbours(b):
            along = [[], [], []]
            mid = [src[z, b] for z in range(3)]
            for z in range(3):
                twice = mid[z] + mid[z]
                along[0].append(
                    twice - (shifted(mid[z], 1, 0, first_x) + shifted(mid[z], -1, 0, last_x))
                )
                along[1].append(
                    twice
                    - (
                        shifted(mid[z], 2 * ZQ, 1, first_y2)
                        + shifted(mid[z], -2 * ZQ, 1, last_y2)
                    )
                )
                below = mid[z - 1] if z > 0 else shifted(mid[2], 2, 1, first_z2)
                above = mid[z + 1] if z < 2 else shifted(mid[0], -2, 1, last_z2)
                along[2].append(twice - (below + above))
            return along

        acc = combine(neighbours, 3)
        return [
            [0.0625 * acc[b][z] + pots_2[z, b] * src[z, b] for z in range(3)] for b in range(BANDS)
        ]

    def split(value):
        high = value.astype(BF16)
        left = value - high.astype(F32)
        middle = left.astype(BF16)
        low = (left - middle.astype(F32)).astype(BF16)
        return jnp.concatenate([high, middle, low], axis=0)

    single = even_y & even_z
    count_2 = 3 * halves * size_x

    def coarse(defect):
        for z in range(3):
            for b in range(8):
                if b < BANDS:
                    value = jnp.where(single, defect[b][z], 0.0)
                else:
                    value = jnp.zeros(plane, F32)
                for h in range(halves):
                    n = (z * halves + h) * size_x
                    cells_2[pl.ds(n * 8 + b, size_x, stride=8), :] = value[
                        :, h * LANES : (h + 1) * LANES
                    ]
        wide = jnp.concatenate(
            [cells_2[pl.ds(n * 8, 8), :] for n in range(count_2)], axis=1
        )
        partial = lax.dot_general(
            onehot[...],
            split(wide),
            (((1,), (1,)), ((), ())),
            preferred_element_type=F32,
        )
        partial = partial[:, :8] + partial[:, 8:16] + partial[:, 16:24]
        acc = [jnp.zeros((8, LANES), F32)] * BANDS
        for b in range(BANDS):
            column = jnp.broadcast_to(partial[:, b : b + 1], (NAGG, LANES))
            for i in range(NAGG // 8):
                for a in range(BANDS):
                    acc[a] = (
                        acc[a]
                        + inverse_ref[b, pl.ds(i * 8, 8), a * LANES : (a + 1) * LANES]
                        * column[i * 8 : (i + 1) * 8]
                    )
        band = iota((8, LANES), 0)
        solved = jnp.zeros((8, LANES), F32)
        for a in range(BANDS):
            solved = jnp.where(band == a, jnp.sum(acc[a], axis=0, keepdims=True), solved)
        spread_out = jnp.dot(
            split(solved[:, :NAGG]), onehot[...], preferred_element_type=F32
        )
        spread_out = spread_out[:8] + spread_out[8:16] + spread_out[16:24]
        for n in range(count_2):
            cells_2[pl.ds(n * 8, 8), :] = spread_out[:, n * LANES : (n + 1) * LANES]

        def correction(b, z):
            parts = [
                cells_2[pl.ds(((z * halves + h) * size_x) * 8 + b, size_x, stride=8), :]
                for h in range(halves)
            ]
            return parts[0] if halves == 1 else jnp.concatenate(parts, axis=1)

        return correction

    def iteration(j, carry):
        factor = scale[...]

        def smooth(x, c_):
            for c in range(COMBOS):
                for b in range(BANDS):
                    value = work[x, c, b] * factor
                    basis[j, x, c, b] = value
                    ext[x + 1, c, b] = winv[x, c, b] * value
            return c_

        lax.fori_loop(0, TX, smooth, 0)
        ghosts()

        def down(x, c_):
            def finish(pair, cells, values):
                for b in range(BANDS):
                    defects = []
                    for n, (yt, zt) in enumerate(cells):
                        residual = basis[j, x, yt * ZT + zt, b]
                        defect = residual - values[b][n]
                        defects.append(defect)
                        work[x, yt * ZT + zt, b] = residual + defect
                    sums[x, pair, b] = (defects[0] + defects[1]) + (defects[2] + defects[3])

            operator_0(x, finish)
            return c_

        lax.fori_loop(0, TX, down, 0)

        for x in range(2):
            for z in range(3):
                for b in range(BANDS):
                    value = 0.125 * (sums[2 * x, z, b] + sums[2 * x + 1, z, b])
                    res_1[x, z, b] = value
                    cor_1[x, z, b] = winv_1[x, z, b] * value

        def defect_1(x, values):
            for b in range(BANDS):
                for z in range(3):
                    value = res_1[x, z, b] - values[b][z]
                    if x == 0:
                        sums[0, z, b] = value
                    else:
                        sums[0, z, b] = sums[0, z, b] + value

        operator_1(cor_1, defect_1)
        for b in range(BANDS):
            for z, value in enumerate(restrict_2([sums[0, z, b] for z in range(3)])):
                res_2[z, b] = value
                cor_2[z, b] = winv_2[z, b] * value
        values = operator_2(cor_2)
        correction = coarse(
            [[res_2[z, b] - values[b][z] for z in range(3)] for b in range(BANDS)]
        )
        for b in range(BANDS):
            for z in range(3):
                cor_2[z, b] = cor_2[z, b] + correction(b, z)
        values = operator_2(cor_2)
        for b in range(BANDS):
            e = [
                cor_2[z, b] + winv_2[z, b] * (res_2[z, b] - values[b][z]) for z in range(3)
            ]
            fine = [
                jnp.where(even_z, e[0], e[1]),
                jnp.where(even_z, e[0], e[2]),
                jnp.where(even_z, e[1], e[2]),
            ]
            for x in range(2):
                for z in range(3):
                    cor_1[x, z, b] = cor_1[x, z, b] + fine[z]

        def post_1(x, values):
            for b in range(BANDS):
                for z in range(3):
                    sums[x, z, b] = cor_1[x, z, b] + winv_1[x, z, b] * (
                        res_1[x, z, b] - values[b][z]
                    )

        operator_1(cor_1, post_1)

        for x in range(2):
            for z in range(3):

                def neighbours(b):
                    mid = sums[x, z, b]
                    near_x = sums[1 - x, z, b]
                    if x == 0:
                        low_x, high_x = shifted(near_x, 1, 0, first_x), near_x
                    else:
                        low_x, high_x = near_x, shifted(near_x, -1, 0, last_x)
                    low_y, high_y = shifted(mid, ZQ, 1, first_y), shifted(mid, -ZQ, 1, last_y)
                    low_z = sums[x, z - 1, b] if z > 0 else shifted(sums[x, 2, b], 1, 1, first_z)
                    high_z = sums[x, z + 1, b] if z < 2 else shifted(sums[x, 0, b], -1, 1, last_z)
                    return [
                        [mid - low_x, mid - high_x],
                        [mid - low_y, mid - high_y],
                        [mid - low_z, mid - high_z],
                    ]

                acc = [None] * 3
                for b in range(BANDS):
                    differences = neighbours(b)
                    for d in range(3):
                        new = []
                        for a in range(BANDS):
                            c = coupling(d, a, b)
                            row = [c * value for value in differences[d]]
                            new.append(
                                row if b == 0 else [acc[d][a][i] + row[i] for i in range(2)]
                            )
                        acc[d] = new
                for d in range(3):
                    for side in range(2):
                        for a in range(BANDS):
                            sides[d, side, x, z, a] = acc[d][a][side]

        def up(x, c_):
            for z in range(3):
                for b in range(BANDS):
                    coarse_value = sums[x // 2, z, b]
                    along_x = sides[0, x % 2, x // 2, z, b]
                    for yt in range(YT):
                        along_xy = along_x + sides[1, yt, x // 2, z, b]
                        for i in range(2):
                            c = yt * ZT + 2 * z + i
                            applied = (
                                along_xy
                                + sides[2, i, x // 2, z, b]
                                + pots[x, c, b] * coarse_value
                            )
                            ext[x + 1, c, b] = coarse_value + winv[x, c, b] * (
                                work[x, c, b] - applied
                            )
            return c_

        lax.fori_loop(0, TX, up, 0)
        ghosts()

        def apply(x, parts):
            parts = list(parts)

            def finish(pair, cells, values):
                for b in range(BANDS):
                    for n, (yt, zt) in enumerate(cells):
                        c = yt * ZT + zt
                        fresh[x, c, b] = values[b][n]
                        for i in range(ITERS):
                            parts[i] = parts[i] + basis[i, x, c, b] * values[b][n]

            operator_0(x, finish)
            quarter = one_lane // GROUP
            for b in range(BANDS):
                for t in range(TILES):
                    merged = None
                    for i in range(4):
                        moved = pltpu.roll(
                            ext[x + 1, t * 4 + i, b], (GROUP * i + lanes - GROUP * my_y) % lanes, 1
                        )[:, :LANES]
                        merged = moved if i == 0 else jnp.where(quarter == i, moved, merged)
                    kept[j, x, b * TILES + t] = merged
            return tuple(parts)

        parts = lax.fori_loop(0, TX, apply, (jnp.zeros(plane, F32),) * ITERS)
        projections = [total_of(part) for part in parts]
        for i in range(ITERS):
            hess[i * ITERS + j] = projections[i]

        def subtract(x, parts):
            parts = list(parts)
            for c in range(COMBOS):
                for b in range(BANDS):
                    n = (c * BANDS + b) % 4
                    value = fresh[x, c, b]
                    for i in range(ITERS):
                        value = value - projections[i] * basis[i, x, c, b]
                    work[x, c, b] = value
                    parts[n] = parts[n] + value * value
            return tuple(parts)

        parts = lax.fori_loop(0, TX, subtract, (jnp.zeros(plane, F32),) * 4)
        total = (parts[0] + parts[1]) + (parts[2] + parts[3])
        norm = jnp.sqrt(total_of(total))
        hess[(j + 1) * ITERS + j] = norm
        scale[...] = 1.0 / norm
        return carry

    lax.fori_loop(0, ITERS, iteration, 0)

    h = [[hess[i * ITERS + j][:, :LANES] for j in range(ITERS)] for i in range(ITERS + 1)]
    normal = [
        [sum(h[i][j] * h[i][k] for i in range(ITERS + 1)) for k in range(ITERS)]
        for j in range(ITERS)
    ]
    first = beta[:, :LANES]
    weights = solve_small(normal, [first * h[0][j] for j in range(ITERS)], ITERS)

    for x in range(TX):
        for b in range(BANDS):
            for t in range(TILES):
                value = weights[0] * kept[0, x, b * TILES + t]
                for j in range(1, ITERS):
                    value = value + weights[j] * kept[j, x, b * TILES + t]
                value = pltpu.roll(value, (size_x - my_g) % size_x, 0)
                row = t * BANDS * TX + b * TX + x
                for z in range(VECS):
                    answer[z, row : row + 1, :] = value[z * groups : z * groups + 1]
    for k in range(VECS):
        outs[k][...] = answer[own ^ k]


def solve_small(normal_matrix, right_side, count):
    factor = {}
    for i in range(count):
        for k in range(i + 1):
            running = normal_matrix[i][k]
            for m in range(k):
                running = running - factor[i, m] * factor[k, m]
            if i == k:
                factor[i, i] = jnp.sqrt(running)
            else:
                factor[i, k] = running / factor[k, k]
    forward = []
    for i in range(count):
        running = right_side[i]
        for k in range(i):
            running = running - factor[i, k] * forward[k]
        forward.append(running / factor[i, i])
    answer = [None] * count
    for i in reversed(range(count)):
        running = forward[i]
        for k in range(i + 1, count):
            running = running - factor[k, i] * answer[k]
        answer[i] = running / factor[i, i]
    return answer


VMEM_SPEC = pl.BlockSpec(memory_space=pltpu.VMEM)
HBM_SPEC = pl.BlockSpec(memory_space=pltpu.HBM)
ANY_SPEC = pl.BlockSpec(memory_space=pl.ANY)
SMEM_SPEC = pl.BlockSpec(memory_space=pltpu.SMEM)


def bits(count):
    return count.bit_length() - 1


def shards(
    size_x, size_y, right_hand, region_labels, potential_table, coupling, aggregate_map,
    coarse_inverse,
):
    groups = size_x // VECS
    devices = size_x * size_y
    names = ("gx", "gy")
    stride = groups * size_y

    def exchanged(value, mask):
        return lax.ppermute(value, names, [(i, i ^ mask) for i in range(devices)])

    row_shape = jax.ShapeDtypeStruct((ROWS, LANES), F32)
    count = BANDS * TX
    packed = pl.pallas_call(
        functools.partial(pack_kernel, groups),
        out_shape=[row_shape] * VECS,
        in_specs=[HBM_SPEC] * 3,
        out_specs=[VMEM_SPEC] * VECS,
        scratch_shapes=[
            pltpu.VMEM((VECS * count + 8, CELLS), F32),
            pltpu.VMEM(right_hand.shape, F32),
            pltpu.VMEM(region_labels.shape, jnp.int32),
            pltpu.VMEM(aggregate_map.shape, jnp.int32),
            pltpu.SemaphoreType.DMA((3,)),
        ],
        compiler_params=pltpu.CompilerParams(vmem_limit_bytes=8 * 2**20),
        name="pack",
    )(right_hand, region_labels, aggregate_map)
    packed, coarse_inverse = lax.optimization_barrier((packed, coarse_inverse))
    parts = [packed[0]] + [exchanged(packed[k], k * stride) for k in range(1, VECS)]
    inverse = pl.pallas_call(
        order_kernel,
        out_shape=jax.ShapeDtypeStruct((BANDS, NAGG, BANDS * LANES), F32),
        in_specs=[VMEM_SPEC],
        out_specs=VMEM_SPEC,
        compiler_params=pltpu.CompilerParams(vmem_limit_bytes=16 * 2**20),
        cost_estimate=pl.CostEstimate(
            flops=6 * (NAGG * BANDS) ** 3, bytes_accessed=2**21, transcendentals=0
        ),
        name="order",
    )(coarse_inverse)

    block, inverse = lax.optimization_barrier((jnp.stack(parts), inverse))
    steps = [("gy", i) for i in range(bits(size_y) - 1, 0, -1)]
    steps += [("gx", i) for i in range(bits(groups))]
    steps += [("gy", 0)]
    pieces = [block]
    for axis, bit in steps:
        mask = (1 << bit) * (size_y if axis == "gx" else 1)
        pieces.append(exchanged(jnp.concatenate(pieces, axis=0), mask))

    lanes = size_y * GROUP
    plane = (size_x, lanes)
    count_2 = 3 * (lanes // LANES) * size_x
    vmem = lambda *shape: pltpu.VMEM(shape + plane, F32)
    scratch = [
        pltpu.VMEM((ROWS, size_y, size_x, LANES), F32),
        vmem(ITERS, TX, COMBOS, BANDS),
        vmem(TX, COMBOS, BANDS),
        vmem(TX + 2, COMBOS, BANDS),
        vmem(TX, COMBOS, BANDS),
        vmem(TX, COMBOS, BANDS),
        vmem(TX, COMBOS, BANDS),
        vmem(TX, 3, BANDS),
        vmem(TX, COMBOS),
        vmem(3),
        pltpu.VMEM((NAGG, count_2 * LANES), BF16),
        vmem(2, 3, BANDS),
        vmem(2, 3, BANDS),
        vmem(3, BANDS),
        vmem(3, BANDS),
        vmem(3, 2, 2, 3, BANDS),
        vmem(2, 3, BANDS),
        vmem(2, 3, BANDS),
        vmem(3, BANDS),
        vmem(3, BANDS),
        pltpu.VMEM((count_2 * 8, LANES), F32),
        pltpu.VMEM((ITERS, TX, BANDS * TILES, size_x, LANES), F32),
        vmem((ITERS + 1) * ITERS),
        vmem(),
        pltpu.VMEM((VECS, FIELD_ROWS, LANES), F32),
        pltpu.SemaphoreType.DMA((devices,)),
    ]
    held = sum(math.prod(ref.shape) * 4 for ref in scratch)
    answers = pl.pallas_call(
        functools.partial(solve_kernel, size_x, size_y, tuple(steps)),
        out_shape=[jax.ShapeDtypeStruct((FIELD_ROWS, LANES), F32)] * VECS,
        in_specs=[ANY_SPEC] * len(pieces) + [SMEM_SPEC, SMEM_SPEC, VMEM_SPEC],
        out_specs=[VMEM_SPEC] * VECS,
        scratch_shapes=scratch,
        compiler_params=pltpu.CompilerParams(
            vmem_limit_bytes=min(held + 6 * 2**20, 63 * 2**20)
        ),
        name="solve",
    )(*pieces, coupling, potential_table, inverse)
    received = [answers[0]] + [exchanged(answers[k], k * stride) for k in range(1, VECS)]
    return pl.pallas_call(
        functools.partial(unpack_kernel, groups),
        out_shape=jax.ShapeDtypeStruct(right_hand.shape, F32),
        in_specs=[VMEM_SPEC] * VECS,
        out_specs=VMEM_SPEC,
        scratch_shapes=[pltpu.VMEM((VECS * count, CELLS), F32)],
        compiler_params=pltpu.CompilerParams(vmem_limit_bytes=8 * 2**20),
        name="unpack",
    )(*received)


def solution(mesh):
    return jax.shard_map(
        functools.partial(shards, mesh.shape["gx"], mesh.shape["gy"]),
        mesh=mesh,
        in_specs=(P(None, None, "gx", "gy"), P("gx", "gy"), P(), P(), P("gx", "gy"), P()),
        out_specs=P(None, None, "gx", "gy"),
        check_vma=False,
    )
```

```python
import functools
import math

import jax
import jax.numpy as jnp
from jax import lax
from jax.experimental import pallas as pl
from jax.experimental.pallas import tpu as pltpu
from jax.sharding import PartitionSpec as P

NZ = 48
BANDS = 6
VECS = 4
REGIONS = 3
ITERS = 3
NAGG = 64
OMEGA = 0.7

HIGHEST = lax.Precision.HIGHEST
F32 = jnp.float32
BF16 = jnp.bfloat16

TX = 4
TY = 8
YT = 2
ZT = 6
COMBOS = YT * ZT
ZQ = NZ // ZT
GROUP = (TY // YT) * ZQ
TILES = 3
FIELD_ROWS = TILES * BANDS * TX
LABEL_ROWS = TILES * TX
AGG_ROW = FIELD_ROWS + LABEL_ROWS
ROWS = 88
LANES = 128
CELLS = TY * NZ
SUBLANES = 8
MIXED = 4 * BANDS * SUBLANES
PARTS = 3 * BANDS * SUBLANES


def source_lane(target):
    combo = target // GROUP
    rest = target % GROUP
    return ((rest // ZQ) * YT + combo // ZT) * NZ + (rest % ZQ) * ZT + combo % ZT


def iota(shape, dim):
    return lax.broadcasted_iota(jnp.int32, shape, dim)


def pack_kernel(groups, right_hbm, labels_hbm, agg_hbm, *rest):
    outs, (stack, right_ref, labels_ref, agg_ref, arrived) = rest[:VECS], rest[VECS:]
    own = lax.axis_index("gx") // groups
    copies = [
        pltpu.make_async_copy(source, target, arrived.at[i])
        for i, (source, target) in enumerate(
            ((right_hbm, right_ref), (labels_hbm, labels_ref), (agg_hbm, agg_ref))
        )
    ]
    for copy in copies:
        copy.start()
    permute = (iota((CELLS, CELLS), 0) == source_lane(iota((1, CELLS), 1))).astype(F32)
    count = BANDS * TX
    for copy in copies:
        copy.wait()
    for k in range(VECS):
        for b in range(BANDS):
            stack[pl.ds(k * count + b * TX, TX), :] = right_ref[own ^ k, b]
    stack[pl.ds(VECS * count, TX), :] = labels_ref[...].astype(F32)
    stack[pl.ds(VECS * count + TX, TX), :] = jnp.zeros((TX, CELLS), F32)
    moved = jnp.dot(stack[...], permute, precision=HIGHEST, preferred_element_type=F32)
    lane = iota((1, LANES), 1)
    inner = lane % GROUP
    wanted = (inner // (2 * ZQ)) * (NZ // 4) + 3 * ((inner % ZQ) // 2) + lane // GROUP
    wanted = jnp.where(lane < 3 * GROUP, wanted, -1)
    cells = agg_ref.shape[1]
    pick = (iota((cells, LANES), 0) == wanted).astype(F32)
    agg = jnp.dot(
        jnp.broadcast_to(agg_ref[...].astype(F32), (8, cells)),
        pick,
        precision=HIGHEST,
        preferred_element_type=F32,
    )
    for k in range(VECS):
        for t in range(TILES):
            tile = slice(t * LANES, (t + 1) * LANES)
            outs[k][pl.ds(t * count, count), :] = moved[k * count : (k + 1) * count, tile]
            outs[k][pl.ds(FIELD_ROWS + t * TX, TX), :] = moved[
                VECS * count : VECS * count + TX, tile
            ]
        outs[k][pl.ds(AGG_ROW, ROWS - AGG_ROW), :] = agg[: ROWS - AGG_ROW]


def unpack_kernel(groups, *refs):
    ins, out_ref, stack = refs[:VECS], refs[VECS], refs[VECS + 1]
    own = lax.axis_index("gx") // groups
    count = BANDS * TX
    permute = (iota((CELLS, CELLS), 1) == source_lane(iota((CELLS, 1), 0))).astype(F32)
    for k in range(VECS):
        for t in range(TILES):
            stack[pl.ds(k * count, count), t * LANES : (t + 1) * LANES] = ins[k][
                pl.ds(t * count, count), :
            ]
    moved = jnp.dot(stack[...], permute, precision=HIGHEST, preferred_element_type=F32)
    for k in range(VECS):
        for b in range(BANDS):
            first = k * count + b * TX
            out_ref[own ^ k, b] = moved[first : first + TX]


def split(value):
    high = value.astype(BF16)
    left = value - high.astype(F32)
    middle = left.astype(BF16)
    return high, middle, (left - middle.astype(F32)).astype(BF16)


def order_kernel(source_ref, out_ref):
    size = NAGG * BANDS
    row, column = iota((size, 1), 0), iota((1, size), 1)
    inputs = (iota((size, size), 1) == (row % NAGG) * BANDS + row // NAGG).astype(F32).astype(BF16)
    outputs = (
        (iota((size, size), 0) == (column % NAGG) * BANDS + column // NAGG).astype(F32).astype(BF16)
    )
    turned = sum(
        lax.dot_general(inputs, part, (((1,), (1,)), ((), ())), preferred_element_type=F32)
        for part in split(source_ref[...])
    )
    ordered = jnp.dot(
        jnp.concatenate(split(turned), axis=0), outputs, preferred_element_type=F32
    )
    out_ref[...] = (ordered[:size] + ordered[size : 2 * size] + ordered[2 * size :]).reshape(
        BANDS, NAGG, size
    )


def solve_kernel(size_x, size_y, places, *refs):
    count = len(places)
    pieces, (coef, table, inverse_ref) = refs[:count], refs[count : count + 3]
    refs = refs[count - 1 :]
    outs = refs[4 : 4 + VECS]
    (
        scratch, basis, fresh, ext, work, pots, winv, sums, labels, aggs, onehot, pots_1, winv_1,
        pots_2, winv_2, sides, weights_f, weights, coupled, coupled_1, res_1, cor_1, res_2, cor_2, cells_2, kept, hess, scale, answer, arrived,
    ) = refs[4 + VECS :]
    groups = size_x // VECS
    lanes = size_y * GROUP
    plane = (size_x, lanes)
    halves = lanes // LANES
    my_x = lax.axis_index("gx")
    my_y = lax.axis_index("gy")
    own = my_x // groups
    my_g = my_x % groups

    sub = iota(plane, 0)
    lane = iota(plane, 1)
    first_x, last_x = sub == 0, sub == size_x - 1
    first_y, last_y = lane < ZQ, lane >= lanes - ZQ
    first_z, last_z = lane % ZQ == 0, lane % ZQ == ZQ - 1

    def shifted(value, amount, axis, mask):
        moved = pltpu.roll(value, amount % value.shape[axis], axis)
        return jnp.where(mask, 0.0, moved)

    def coupling(direction, a, b):
        return coef[direction, a, b]

    def centre(band):
        return 2.0 * (coupling(0, band, band) + coupling(1, band, band) + coupling(2, band, band))

    narrow = plane == (SUBLANES, LANES)
    copies = []
    for piece, blocks in zip(pieces, places):
        for i, (k, mask_g, mask_y) in enumerate(blocks):
            other_x, other_y = (own ^ k) * groups + (my_g ^ mask_g), my_y ^ mask_y
            if narrow:
                first = other_y * size_x + other_x
                scratch[pl.ds(first, ROWS, stride=size_x * size_y), :] = piece[i]
            else:
                target = scratch.at[:, other_y, other_x, :]
                copies.append(pltpu.make_async_copy(piece.at[i], target, arrived.at[len(copies)]))
    for copy in copies:
        copy.start()

    if narrow:
        row = iota((SUBLANES, PARTS), 0)
        column = iota((SUBLANES, PARTS), 1)
        band, part = (column // SUBLANES) % BANDS, column // (BANDS * SUBLANES)
        same = column % SUBLANES == row
        for a in range(BANDS):
            rows = [jnp.zeros((SUBLANES, PARTS), F32)] * 3
            for b in range(BANDS):
                rows = [jnp.where(band == b, coupling(d, a, b), rows[d]) for d in range(3)]
            rows = [2.0 * (rows[0] + rows[1] + rows[2])] + [-value for value in rows]
            for g, value in enumerate(rows):
                value = jnp.where(same, value, 0.0)
                high = value.astype(BF16).astype(F32)
                weights_f[pl.ds((g * BANDS + a) * SUBLANES, SUBLANES), :] = jnp.where(
                    part < 2, high, value - high
                )
        weights[...] = weights_f[...].astype(BF16)

    def mix(columns):
        parts = []
        for values in columns:
            value = jnp.concatenate(values, axis=0)
            high = value.astype(BF16)
            low = (value - high.astype(F32)).astype(BF16)
            parts.append(jnp.concatenate([high, low, high], axis=0))
        return jnp.dot(
            weights[...], jnp.concatenate(parts, axis=1), preferred_element_type=F32
        )

    def block_of(g, a, n):
        first = (g * BANDS + a) * SUBLANES
        return slice(first, first + SUBLANES), slice(n * LANES, (n + 1) * LANES)

    one_lane = iota((size_x, LANES), 1)
    low_64, low_32 = one_lane < 64, one_lane % 64 < 32

    def regroup(row):
        result = []
        for h in range(halves):
            if narrow:
                first = row * size_y * size_x
                g = [scratch[pl.ds(first + i * size_x, size_x), :] for i in range(4)]
            else:
                g = [scratch[row, 4 * h + i] for i in range(4)]
            for i in (0, 1):
                low, high = g[i], g[i + 2]
                g[i] = jnp.where(low_64, low, pltpu.roll(high, 64, 1))
                g[i + 2] = jnp.where(low_64, pltpu.roll(low, 64, 1), high)
            for i in (0, 2):
                low, high = g[i], g[i + 1]
                g[i] = jnp.where(low_32, low, pltpu.roll(high, 32, 1))
                g[i + 1] = jnp.where(low_32, pltpu.roll(low, 96, 1), high)
            result.append(g)
        return [
            result[0][c] if halves == 1 else jnp.concatenate([r[c] for r in result], axis=1)
            for c in range(4)
        ]

    def load_field(x, total):
        for t in range(TILES):
            for b in range(BANDS):
                for c, value in enumerate(regroup(t * BANDS * TX + b * TX + x)):
                    work[x, t * 4 + c, b] = value
                    for i in range(1, ITERS):
                        basis[i, x, t * 4 + c, b] = jnp.zeros(plane, F32)
                    total = total + value * value
            for c, value in enumerate(regroup(FIELD_ROWS + t * TX + x)):
                labels[x, t * 4 + c] = value
        return total

    for copy in copies:
        copy.wait()
    total = lax.fori_loop(0, TX, load_field, jnp.zeros(plane, F32))
    for k, value in enumerate(regroup(AGG_ROW)[:3]):
        aggs[k] = value

    def total_of(value):
        return jnp.broadcast_to(jnp.sum(value, keepdims=True), plane)

    for i in range((ITERS + 1) * ITERS):
        hess[i] = jnp.zeros(plane, F32)

    def fill(x, carry):
        for b in range(BANDS):
            diagonal = centre(b)
            for zt in range(ZT):
                for yt in range(YT):
                    label = labels[x, yt * ZT + zt]
                    value = jnp.zeros(plane, F32)
                    for r in range(REGIONS):
                        value = jnp.where(label == float(r), table[r, b], value)
                    pots[x, yt * ZT + zt, b] = value
                    winv[x, yt * ZT + zt, b] = OMEGA * (1.0 / (diagonal + value))
                    if zt % 2 == 0 and yt == 0:
                        four = value
                    else:
                        four = four + value
                if zt % 2 == 1:
                    sums[x, zt // 2, b] = four
        return carry

    lax.fori_loop(0, TX, fill, 0)

    even_z = lane % 2 == 0
    even_y = (lane // ZQ) % 2 == 0

    def restrict_2(q):
        near, far = q[0] + q[1], q[1] + q[2]
        p = [
            jnp.where(even_z, near, pltpu.roll(near, 1, 1)),
            jnp.where(even_z, q[2], q[0])
            + jnp.where(even_z, pltpu.roll(q[0], lanes - 1, 1), pltpu.roll(q[2], 1, 1)),
            jnp.where(even_z, pltpu.roll(far, lanes - 1, 1), far),
        ]
        return [
            0.125
            * (v + jnp.where(even_y, pltpu.roll(v, lanes - ZQ, 1), pltpu.roll(v, ZQ, 1)))
            for v in p
        ]

    for b in range(BANDS):
        q = []
        for z in range(3):
            pair = []
            for x in range(2):
                value = 0.125 * (sums[2 * x, z, b] + sums[2 * x + 1, z, b])
                pots_1[x, z, b] = value
                winv_1[x, z, b] = OMEGA * (1.0 / (0.25 * centre(b) + value))
                pair.append(value)
            q.append(pair[0] + pair[1])
        for k, value in enumerate(restrict_2(q)):
            pots_2[k, b] = value
            winv_2[k, b] = OMEGA * (1.0 / (0.0625 * centre(b) + value))

    for k in range(3):
        for h in range(halves):
            for x in range(size_x):
                n = (k * halves + h) * size_x + x
                row = aggs[k, x : x + 1, h * LANES : (h + 1) * LANES]
                onehot[:, n * LANES : (n + 1) * LANES] = (
                    (row == iota((NAGG, LANES), 0).astype(F32)).astype(F32).astype(BF16)
                )

    beta = jnp.sqrt(total_of(total))
    scale[...] = 1.0 / beta

    def ghosts():
        for c in range(COMBOS):
            for b in range(BANDS):
                if narrow:
                    rows, columns = block_of(1, b, c)
                    coupled[TX + 1, rows, columns] = shifted(coupled[1, rows, columns], -1, 0, last_x)
                    coupled[0, rows, columns] = shifted(coupled[TX, rows, columns], 1, 0, first_x)
                    continue
                ext[TX + 1, c, b] = shifted(ext[1, c, b], -1, 0, last_x)
                ext[0, c, b] = shifted(ext[TX, c, b], 1, 0, first_x)

    def combine(neighbours, count):
        acc = None
        for b in range(BANDS):
            differences = neighbours(b)
            new = []
            for a in range(BANDS):
                c = [coupling(d, a, b) for d in range(3)]
                row = []
                for n in range(count):
                    value = c[0] * differences[0][n]
                    value = value + c[1] * differences[1][n]
                    value = value + c[2] * differences[2][n]
                    row.append(value if acc is None else acc[a][n] + value)
                new.append(row)
            acc = new
        return acc

    def mix_some(x, c, row, columns):
        if not narrow:
            return
        columns.append(row)
        if len(columns) == 4:
            coupled[x + 1, :, (c - 3) * LANES : (c + 1) * LANES] = mix(columns)
            columns.clear()

    def mixed_0(x, cells):
        def at(g, a, yt, zt, dx=0):
            rows, columns = block_of(g, a, yt * ZT + zt)
            return coupled[x + 1 + dx, rows, columns]

        values = []
        for a in range(BANDS):
            row = []
            for yt, zt in cells:
                value = at(0, a, yt, zt) + (at(1, a, yt, zt, 1) + at(1, a, yt, zt, -1))
                partner = at(2, a, 1 - yt, zt)
                if yt == 0:
                    outer = shifted(partner, ZQ, 1, first_y)
                else:
                    outer = shifted(partner, -ZQ, 1, last_y)
                value = value + (partner + outer)
                if zt == 0:
                    below = shifted(at(3, a, yt, ZT - 1), 1, 1, first_z)
                else:
                    below = at(3, a, yt, zt - 1)
                if zt == ZT - 1:
                    above = shifted(at(3, a, yt, 0), -1, 1, last_z)
                else:
                    above = at(3, a, yt, zt + 1)
                value = value + (below + above)
                row.append(value + pots[x, yt * ZT + zt, a] * ext[x + 1, yt * ZT + zt, a])
            values.append(row)
        return values

    def mix_1(src):
        coupled_1[...] = mix([[src[x, z, b] for b in range(BANDS)] for x in range(2) for z in range(3)])

        def sides_of(d, a, x, z):
            def at(x, z):
                return coupled_1[block_of(d + 1, a, x * 3 + z)]

            mid = at(x, z)
            if d == 0:
                other = at(1 - x, z)
                if x == 0:
                    return mid, shifted(other, 1, 0, first_x), other
                return mid, other, shifted(other, -1, 0, last_x)
            if d == 1:
                return mid, shifted(mid, ZQ, 1, first_y), shifted(mid, -ZQ, 1, last_y)
            below = at(x, z - 1) if z > 0 else shifted(at(x, 2), 1, 1, first_z)
            above = at(x, z + 1) if z < 2 else shifted(at(x, 0), -1, 1, last_z)
            return mid, below, above

        return sides_of

    def operator_0(x, finish):
        for pair in range(ZT // 2):
            cells = [(yt, 2 * pair + i) for i in range(2) for yt in range(YT)]
            if narrow:
                finish(pair, cells, mixed_0(x, cells))
                continue

            def neighbours(b):
                def at(dx, yt, zt):
                    return ext[x + 1 + dx, yt * ZT + zt, b]

                mid = {cell: at(0, *cell) for cell in cells}
                along = [[], [], []]
                for yt, zt in cells:
                    twice = mid[yt, zt] + mid[yt, zt]
                    along[0].append(twice - (at(1, yt, zt) + at(-1, yt, zt)))
                    partner = mid[1 - yt, zt]
                    if yt == 0:
                        outer = shifted(partner, ZQ, 1, first_y)
                    else:
                        outer = shifted(partner, -ZQ, 1, last_y)
                    along[1].append(twice - (partner + outer))
                    if zt % 2 == 0:
                        inside = mid[yt, zt + 1]
                        if zt == 0:
                            outer = shifted(at(0, yt, ZT - 1), 1, 1, first_z)
                        else:
                            outer = at(0, yt, zt - 1)
                    else:
                        inside = mid[yt, zt - 1]
                        if zt == ZT - 1:
                            outer = shifted(at(0, yt, 0), -1, 1, last_z)
                        else:
                            outer = at(0, yt, zt + 1)
                    along[2].append(twice - (inside + outer))
                return along

            acc = combine(neighbours, len(cells))
            values = [
                [
                    acc[b][n] + pots[x, yt * ZT + zt, b] * ext[x + 1, yt * ZT + zt, b]
                    for n, (yt, zt) in enumerate(cells)
                ]
                for b in range(BANDS)
            ]
            finish(pair, cells, values)

    def operator_1(src, finish):
        for x in range(2):

            def neighbours(b):
                along = [[], [], []]
                mid = [src[x, z, b] for z in range(3)]
                for z in range(3):
                    twice = mid[z] + mid[z]
                    partner = src[1 - x, z, b]
                    if x == 0:
                        outer = shifted(partner, 1, 0, first_x)
                    else:
                        outer = shifted(partner, -1, 0, last_x)
                    along[0].append(twice - (partner + outer))
                    along[1].append(
                        twice
                        - (shifted(mid[z], ZQ, 1, first_y) + shifted(mid[z], -ZQ, 1, last_y))
                    )
                    below = mid[z - 1] if z > 0 else shifted(mid[2], 1, 1, first_z)
                    above = mid[z + 1] if z < 2 else shifted(mid[0], -1, 1, last_z)
                    along[2].append(twice - (below + above))
                return along

            acc = combine(neighbours, 3)
            finish(
                x,
                [
                    [0.25 * acc[b][z] + pots_1[x, z, b] * src[x, z, b] for z in range(3)]
                    for b in range(BANDS)
                ],
            )

    first_y2, last_y2 = lane < 2 * ZQ, lane >= lanes - 2 * ZQ
    first_z2, last_z2 = lane % ZQ < 2, lane % ZQ >= ZQ - 2

    def operator_2(src):
        def neighbours(b):
            along = [[], [], []]
            mid = [src[z, b] for z in range(3)]
            for z in range(3):
                twice = mid[z] + mid[z]
                along[0].append(
                    twice - (shifted(mid[z], 1, 0, first_x) + shifted(mid[z], -1, 0, last_x))
                )
                along[1].append(
                    twice
                    - (
                        shifted(mid[z], 2 * ZQ, 1, first_y2)
                        + shifted(mid[z], -2 * ZQ, 1, last_y2)
                    )
                )
                below = mid[z - 1] if z > 0 else shifted(mid[2], 2, 1, first_z2)
                above = mid[z + 1] if z < 2 else shifted(mid[0], -2, 1, last_z2)
                along[2].append(twice - (below + above))
            return along

        acc = combine(neighbours, 3)
        return [
            [0.0625 * acc[b][z] + pots_2[z, b] * src[z, b] for z in range(3)] for b in range(BANDS)
        ]

    single = even_y & even_z
    count_2 = 3 * halves * size_x

    def coarse(defect):
        for z in range(3):
            for b in range(8):
                if b < BANDS:
                    value = jnp.where(single, defect[b][z], 0.0)
                else:
                    value = jnp.zeros(plane, F32)
                for h in range(halves):
                    n = (z * halves + h) * size_x
                    cells_2[pl.ds(n * 8 + b, size_x, stride=8), :] = value[
                        :, h * LANES : (h + 1) * LANES
                    ]
        wide = jnp.concatenate(
            [cells_2[pl.ds(n * 8, 8), :] for n in range(count_2)], axis=1
        )
        partial = lax.dot_general(
            onehot[...],
            jnp.concatenate(split(wide), axis=0),
            (((1,), (1,)), ((), ())),
            preferred_element_type=F32,
        )
        partial = partial[:, :8] + partial[:, 8:16] + partial[:, 16:24]
        pairs = NAGG * BANDS // LANES
        acc = [jnp.zeros((8, LANES), F32)] * pairs
        for b in range(BANDS):
            column = jnp.broadcast_to(partial[:, b : b + 1], (NAGG, LANES))
            for i in range(NAGG // 8):
                for a in range(pairs):
                    acc[a] = (
                        acc[a]
                        + inverse_ref[b, pl.ds(i * 8, 8), a * LANES : (a + 1) * LANES]
                        * column[i * 8 : (i + 1) * 8]
                    )
        band = iota((8, LANES), 0)
        solved = jnp.zeros((8, LANES), F32)
        for a in range(pairs):
            both = jnp.broadcast_to(jnp.sum(acc[a], axis=0, keepdims=True), (8, LANES))
            solved = jnp.where(band == 2 * a, both, solved)
            solved = jnp.where(band == 2 * a + 1, pltpu.roll(both, NAGG, 1), solved)
        spread_out = jnp.dot(
            jnp.concatenate(split(solved[:, :NAGG]), axis=0), onehot[...], preferred_element_type=F32
        )
        spread_out = spread_out[:8] + spread_out[8:16] + spread_out[16:24]
        for n in range(count_2):
            cells_2[pl.ds(n * 8, 8), :] = spread_out[:, n * LANES : (n + 1) * LANES]

        def correction(b, z):
            parts = [
                cells_2[pl.ds(((z * halves + h) * size_x) * 8 + b, size_x, stride=8), :]
                for h in range(halves)
            ]
            return parts[0] if halves == 1 else jnp.concatenate(parts, axis=1)

        return correction

    def prolonged_sides():
        for x in range(2):
            for z in range(3):

                def neighbours(b):
                    mid = sums[x, z, b]
                    near_x = sums[1 - x, z, b]
                    if x == 0:
                        low_x, high_x = shifted(near_x, 1, 0, first_x), near_x
                    else:
                        low_x, high_x = near_x, shifted(near_x, -1, 0, last_x)
                    low_y, high_y = shifted(mid, ZQ, 1, first_y), shifted(mid, -ZQ, 1, last_y)
                    low_z = sums[x, z - 1, b] if z > 0 else shifted(sums[x, 2, b], 1, 1, first_z)
                    high_z = sums[x, z + 1, b] if z < 2 else shifted(sums[x, 0, b], -1, 1, last_z)
                    return [
                        [mid - low_x, mid - high_x],
                        [mid - low_y, mid - high_y],
                        [mid - low_z, mid - high_z],
                    ]

                acc = [None] * 3
                for b in range(BANDS):
                    differences = neighbours(b)
                    for d in range(3):
                        new = []
                        for a in range(BANDS):
                            c = coupling(d, a, b)
                            row = [c * value for value in differences[d]]
                            new.append(
                                row if b == 0 else [acc[d][a][i] + row[i] for i in range(2)]
                            )
                        acc[d] = new
                for d in range(3):
                    for side in range(2):
                        for a in range(BANDS):
                            sides[d, side, x, z, a] = acc[d][a][side]

    def over_x(body, carry):
        if not narrow:
            return lax.fori_loop(0, TX, body, carry)
        for x in range(TX):
            carry = body(x, carry)
        return carry

    def iteration(j, carry):
        factor = scale[...]

        def smooth(x, c_):
            columns = []
            for c in range(COMBOS):
                row = []
                for b in range(BANDS):
                    value = work[x, c, b] * factor
                    basis[j, x, c, b] = value
                    value = winv[x, c, b] * value
                    ext[x + 1, c, b] = value
                    row.append(value)
                mix_some(x, c, row, columns)
            return c_

        over_x(smooth, 0)
        ghosts()

        def down(x, c_):
            def finish(pair, cells, values):
                for b in range(BANDS):
                    defects = []
                    for n, (yt, zt) in enumerate(cells):
                        residual = basis[j, x, yt * ZT + zt, b]
                        defect = residual - values[b][n]
                        defects.append(defect)
                        work[x, yt * ZT + zt, b] = residual + defect
                    sums[x, pair, b] = (defects[0] + defects[1]) + (defects[2] + defects[3])

            operator_0(x, finish)
            return c_

        over_x(down, 0)

        for x in range(2):
            for z in range(3):
                for b in range(BANDS):
                    value = 0.125 * (sums[2 * x, z, b] + sums[2 * x + 1, z, b])
                    res_1[x, z, b] = value
                    cor_1[x, z, b] = winv_1[x, z, b] * value

        def defect_1(x, values):
            for b in range(BANDS):
                for z in range(3):
                    value = res_1[x, z, b] - values[b][z]
                    if x == 0:
                        sums[0, z, b] = value
                    else:
                        sums[0, z, b] = sums[0, z, b] + value

        operator_1(cor_1, defect_1)
        for b in range(BANDS):
            for z, value in enumerate(restrict_2([sums[0, z, b] for z in range(3)])):
                res_2[z, b] = value
                cor_2[z, b] = winv_2[z, b] * value
        values = operator_2(cor_2)
        correction = coarse(
            [[res_2[z, b] - values[b][z] for z in range(3)] for b in range(BANDS)]
        )
        for b in range(BANDS):
            for z in range(3):
                cor_2[z, b] = cor_2[z, b] + correction(b, z)
        values = operator_2(cor_2)
        for b in range(BANDS):
            e = [
                cor_2[z, b] + winv_2[z, b] * (res_2[z, b] - values[b][z]) for z in range(3)
            ]
            fine = [
                jnp.where(even_z, e[0], e[1]),
                jnp.where(even_z, e[0], e[2]),
                jnp.where(even_z, e[1], e[2]),
            ]
            for x in range(2):
                for z in range(3):
                    cor_1[x, z, b] = cor_1[x, z, b] + fine[z]

        def post_1(x, values):
            for b in range(BANDS):
                for z in range(3):
                    sums[x, z, b] = cor_1[x, z, b] + winv_1[x, z, b] * (
                        res_1[x, z, b] - values[b][z]
                    )

        operator_1(cor_1, post_1)

        if narrow:
            sides_of = mix_1(sums)
            for d in range(3):
                for x in range(2):
                    for z in range(3):
                        for a in range(BANDS):
                            mid, low, high = sides_of(d, a, x, z)
                            sides[d, 0, x, z, a] = low - mid
                            sides[d, 1, x, z, a] = high - mid
        else:
            prolonged_sides()

        def up(x, c_):
            columns = []
            for yt in range(YT):
                for zt in range(ZT):
                    z, c = zt // 2, yt * ZT + zt
                    row = []
                    for b in range(BANDS):
                        coarse_value = sums[x // 2, z, b]
                        applied = (
                            (sides[0, x % 2, x // 2, z, b] + sides[1, yt, x // 2, z, b])
                            + sides[2, zt % 2, x // 2, z, b]
                            + pots[x, c, b] * coarse_value
                        )
                        value = coarse_value + winv[x, c, b] * (work[x, c, b] - applied)
                        ext[x + 1, c, b] = value
                        row.append(value)
                    mix_some(x, c, row, columns)
            return c_

        over_x(up, 0)
        ghosts()

        def apply(x, parts):
            parts = list(parts)

            def finish(pair, cells, values):
                for b in range(BANDS):
                    for n, (yt, zt) in enumerate(cells):
                        c = yt * ZT + zt
                        fresh[x, c, b] = values[b][n]
                        for i in range(ITERS):
                            parts[i] = parts[i] + basis[i, x, c, b] * values[b][n]

            operator_0(x, finish)
            quarter = one_lane // GROUP
            for b in range(BANDS):
                for t in range(TILES):
                    merged = None
                    for i in range(4):
                        moved = pltpu.roll(
                            ext[x + 1, t * 4 + i, b], (GROUP * i + lanes - GROUP * my_y) % lanes, 1
                        )[:, :LANES]
                        merged = moved if i == 0 else jnp.where(quarter == i, moved, merged)
                    kept[j, x, b * TILES + t] = merged
            return tuple(parts)

        parts = over_x(apply, (jnp.zeros(plane, F32),) * ITERS)
        projections = [total_of(part) for part in parts]
        for i in range(ITERS):
            hess[i * ITERS + j] = projections[i]

        def subtract(x, parts):
            parts = list(parts)
            for c in range(COMBOS):
                for b in range(BANDS):
                    n = (c * BANDS + b) % 4
                    value = fresh[x, c, b]
                    for i in range(ITERS):
                        value = value - projections[i] * basis[i, x, c, b]
                    work[x, c, b] = value
                    parts[n] = parts[n] + value * value
            return tuple(parts)

        parts = lax.fori_loop(0, TX, subtract, (jnp.zeros(plane, F32),) * 4)
        total = (parts[0] + parts[1]) + (parts[2] + parts[3])
        norm = jnp.sqrt(total_of(total))
        hess[(j + 1) * ITERS + j] = norm
        scale[...] = 1.0 / norm
        return carry

    lax.fori_loop(0, ITERS, iteration, 0)

    h = [[hess[i * ITERS + j][:, :LANES] for j in range(ITERS)] for i in range(ITERS + 1)]
    normal = [
        [sum(h[i][j] * h[i][k] for i in range(ITERS + 1)) for k in range(ITERS)]
        for j in range(ITERS)
    ]
    first = beta[:, :LANES]
    weights = solve_small(normal, [first * h[0][j] for j in range(ITERS)], ITERS)

    for x in range(TX):
        for b in range(BANDS):
            for t in range(TILES):
                value = weights[0] * kept[0, x, b * TILES + t]
                for j in range(1, ITERS):
                    value = value + weights[j] * kept[j, x, b * TILES + t]
                value = pltpu.roll(value, (size_x - my_g) % size_x, 0)
                row = t * BANDS * TX + b * TX + x
                for z in range(VECS):
                    answer[z, row : row + 1, :] = value[z * groups : z * groups + 1]
    for k in range(VECS):
        outs[k][...] = answer[own ^ k]


def solve_small(normal_matrix, right_side, count):
    factor = {}
    for i in range(count):
        for k in range(i + 1):
            running = normal_matrix[i][k]
            for m in range(k):
                running = running - factor[i, m] * factor[k, m]
            if i == k:
                factor[i, i] = jnp.sqrt(running)
            else:
                factor[i, k] = running / factor[k, k]
    forward = []
    for i in range(count):
        running = right_side[i]
        for k in range(i):
            running = running - factor[i, k] * forward[k]
        forward.append(running / factor[i, i])
    answer = [None] * count
    for i in reversed(range(count)):
        running = forward[i]
        for k in range(i + 1, count):
            running = running - factor[k, i] * answer[k]
        answer[i] = running / factor[i, i]
    return answer


VMEM_SPEC = pl.BlockSpec(memory_space=pltpu.VMEM)
HBM_SPEC = pl.BlockSpec(memory_space=pltpu.HBM)
ANY_SPEC = pl.BlockSpec(memory_space=pl.ANY)
SMEM_SPEC = pl.BlockSpec(memory_space=pltpu.SMEM)


def bits(count):
    return count.bit_length() - 1


def shards(
    size_x, size_y, right_hand, region_labels, potential_table, coupling, aggregate_map,
    coarse_inverse,
):
    groups = size_x // VECS
    devices = size_x * size_y
    names = ("gx", "gy")
    stride = groups * size_y

    def exchanged(value, mask):
        return lax.ppermute(value, names, [(i, i ^ mask) for i in range(devices)])

    row_shape = jax.ShapeDtypeStruct((ROWS, LANES), F32)
    count = BANDS * TX
    packed = pl.pallas_call(
        functools.partial(pack_kernel, groups),
        out_shape=[row_shape] * VECS,
        in_specs=[HBM_SPEC] * 3,
        out_specs=[VMEM_SPEC] * VECS,
        scratch_shapes=[
            pltpu.VMEM((VECS * count + 8, CELLS), F32),
            pltpu.VMEM(right_hand.shape, F32),
            pltpu.VMEM(region_labels.shape, jnp.int32),
            pltpu.VMEM(aggregate_map.shape, jnp.int32),
            pltpu.SemaphoreType.DMA((3,)),
        ],
        compiler_params=pltpu.CompilerParams(vmem_limit_bytes=60 * 2**20),
        name="pack",
    )(right_hand, region_labels, aggregate_map)
    packed, coarse_inverse = lax.optimization_barrier((packed, coarse_inverse))
    parts = [packed[0]] + [exchanged(packed[k], k * stride) for k in range(1, VECS)]
    inverse = pl.pallas_call(
        order_kernel,
        out_shape=jax.ShapeDtypeStruct((BANDS, NAGG, BANDS * NAGG), F32),
        in_specs=[VMEM_SPEC],
        out_specs=VMEM_SPEC,
        compiler_params=pltpu.CompilerParams(vmem_limit_bytes=16 * 2**20),
        cost_estimate=pl.CostEstimate(
            flops=6 * (NAGG * BANDS) ** 3, bytes_accessed=2**21, transcendentals=0
        ),
        name="order",
    )(coarse_inverse)

    steps = [("gy", i) for i in range(bits(size_y) - 1, 0, -1)]
    steps += [("gx", i) for i in range(bits(groups))]
    second, inverse = lax.optimization_barrier((jnp.stack(parts[2:]), inverse))
    halves = [[jnp.stack(parts[:2])], [second]]
    places = [[[(k, 0, 0) for k in (0, 1)]], [[(k, 0, 0) for k in (2, 3)]]]

    def widen(half, axis, bit):
        mask = 1 << bit
        sent = halves[half][0] if len(halves[half]) == 1 else jnp.concatenate(halves[half])
        halves[half].append(exchanged(sent, mask * (size_y if axis == "gx" else 1)))
        mask_g, mask_y = (mask, 0) if axis == "gx" else (0, mask)
        places[half].append(
            [(k, g ^ mask_g, y ^ mask_y) for blocks in places[half] for k, g, y in blocks]
        )

    for first, last in zip(steps, steps[::-1]):
        widen(0, *first)
        widen(1, *last)
    widen(0, "gy", 0)
    widen(1, "gy", 0)
    pieces = halves[0] + halves[1]
    places = places[0] + places[1]

    lanes = size_y * GROUP
    plane = (size_x, lanes)
    count_2 = 3 * (lanes // LANES) * size_x
    narrow = plane == (SUBLANES, LANES)
    vmem = lambda *shape: pltpu.VMEM(shape + plane, F32)
    scratch = [
        pltpu.VMEM((ROWS * devices, LANES) if narrow else (ROWS, size_y, size_x, LANES), F32),
        vmem(ITERS, TX, COMBOS, BANDS),
        vmem(TX, COMBOS, BANDS),
        vmem(TX + 2, COMBOS, BANDS),
        vmem(TX, COMBOS, BANDS),
        vmem(TX, COMBOS, BANDS),
        vmem(TX, COMBOS, BANDS),
        vmem(TX, 3, BANDS),
        vmem(TX, COMBOS),
        vmem(3),
        pltpu.VMEM((NAGG, count_2 * LANES), BF16),
        vmem(2, 3, BANDS),
        vmem(2, 3, BANDS),
        vmem(3, BANDS),
        vmem(3, BANDS),
        vmem(3, 2, 2, 3, BANDS),
        pltpu.VMEM((MIXED, PARTS), F32),
        pltpu.VMEM((MIXED, PARTS), BF16),
        pltpu.VMEM((TX + 2, MIXED, COMBOS * LANES) if narrow else (8, LANES), F32),
        pltpu.VMEM((MIXED, 2 * TILES * LANES), F32),
        vmem(2, 3, BANDS),
        vmem(2, 3, BANDS),
        vmem(3, BANDS),
        vmem(3, BANDS),
        pltpu.VMEM((count_2 * 8, LANES), F32),
        pltpu.VMEM((ITERS, TX, BANDS * TILES, size_x, LANES), F32),
        vmem((ITERS + 1) * ITERS),
        vmem(),
        pltpu.VMEM((VECS, FIELD_ROWS, LANES), F32),
        pltpu.SemaphoreType.DMA((devices,)),
    ]
    held = sum(math.prod(ref.shape) * 4 for ref in scratch)
    answers = pl.pallas_call(
        functools.partial(solve_kernel, size_x, size_y, places),
        out_shape=[jax.ShapeDtypeStruct((FIELD_ROWS, LANES), F32)] * VECS,
        in_specs=[VMEM_SPEC if narrow else ANY_SPEC] * len(pieces) + [SMEM_SPEC, SMEM_SPEC, VMEM_SPEC],
        out_specs=[VMEM_SPEC] * VECS,
        scratch_shapes=scratch,
        compiler_params=pltpu.CompilerParams(
            vmem_limit_bytes=min(held + 6 * 2**20, 63 * 2**20)
        ),
        name="solve",
    )(*pieces, coupling, potential_table, inverse)
    received = [answers[0]] + [exchanged(answers[k], k * stride) for k in range(1, VECS)]
    return pl.pallas_call(
        functools.partial(unpack_kernel, groups),
        out_shape=jax.ShapeDtypeStruct(right_hand.shape, F32),
        in_specs=[VMEM_SPEC] * VECS,
        out_specs=VMEM_SPEC,
        scratch_shapes=[pltpu.VMEM((VECS * count, CELLS), F32)],
        compiler_params=pltpu.CompilerParams(vmem_limit_bytes=8 * 2**20),
        name="unpack",
    )(*received)


def solution(mesh):
    return jax.shard_map(
        functools.partial(shards, mesh.shape["gx"], mesh.shape["gy"]),
        mesh=mesh,
        in_specs=(P(None, None, "gx", "gy"), P("gx", "gy"), P(), P(), P("gx", "gy"), P()),
        out_specs=P(None, None, "gx", "gy"),
        check_vma=False,
    )
```

```python
import functools
import math

import jax
import jax.numpy as jnp
from jax import lax
from jax.experimental import pallas as pl
from jax.experimental.pallas import tpu as pltpu
from jax.sharding import PartitionSpec as P

NZ = 48
BANDS = 6
VECS = 4
REGIONS = 3
ITERS = 3
NAGG = 64
OMEGA = 0.7

HIGHEST = lax.Precision.HIGHEST
F32 = jnp.float32
BF16 = jnp.bfloat16

TX = 4
TY = 8
YT = 2
ZT = 6
COMBOS = YT * ZT
ZQ = NZ // ZT
GROUP = (TY // YT) * ZQ
TILES = 3
FIELD_ROWS = TILES * BANDS * TX
LABEL_ROWS = TILES * TX
AGG_ROW = FIELD_ROWS + LABEL_ROWS
ROWS = 88
LANES = 128
CELLS = TY * NZ
SUBLANES = 8
MIXED = 4 * BANDS * SUBLANES
PARTS = 3 * BANDS * SUBLANES


def source_lane(target):
    combo = target // GROUP
    rest = target % GROUP
    return ((rest // ZQ) * YT + combo // ZT) * NZ + (rest % ZQ) * ZT + combo % ZT


def iota(shape, dim):
    return lax.broadcasted_iota(jnp.int32, shape, dim)


def pack_kernel(groups, right_hbm, labels_hbm, agg_hbm, *rest):
    outs, (stack, right_ref, labels_ref, agg_ref, arrived) = rest[:VECS], rest[VECS:]
    own = lax.axis_index("gx") // groups
    copies = [
        pltpu.make_async_copy(source, target, arrived.at[i])
        for i, (source, target) in enumerate(
            ((right_hbm, right_ref), (labels_hbm, labels_ref), (agg_hbm, agg_ref))
        )
    ]
    for copy in copies:
        copy.start()
    permute = (iota((CELLS, CELLS), 0) == source_lane(iota((1, CELLS), 1))).astype(F32)
    count = BANDS * TX
    for copy in copies:
        copy.wait()
    for k in range(VECS):
        for b in range(BANDS):
            stack[pl.ds(k * count + b * TX, TX), :] = right_ref[own ^ k, b]
    stack[pl.ds(VECS * count, TX), :] = labels_ref[...].astype(F32)
    stack[pl.ds(VECS * count + TX, TX), :] = jnp.zeros((TX, CELLS), F32)
    moved = sum(
        jnp.dot(part, permute.astype(BF16), preferred_element_type=F32) for part in split(stack[...])
    )
    lane = iota((1, LANES), 1)
    inner = lane % GROUP
    wanted = (inner // (2 * ZQ)) * (NZ // 4) + 3 * ((inner % ZQ) // 2) + lane // GROUP
    wanted = jnp.where(lane < 3 * GROUP, wanted, -1)
    cells = agg_ref.shape[1]
    pick = (iota((cells, LANES), 0) == wanted).astype(F32)
    agg = jnp.dot(
        jnp.broadcast_to(agg_ref[...].astype(F32), (8, cells)),
        pick,
        precision=HIGHEST,
        preferred_element_type=F32,
    )
    for k in range(VECS):
        for t in range(TILES):
            tile = slice(t * LANES, (t + 1) * LANES)
            outs[k][pl.ds(t * count, count), :] = moved[k * count : (k + 1) * count, tile]
            outs[k][pl.ds(FIELD_ROWS + t * TX, TX), :] = moved[
                VECS * count : VECS * count + TX, tile
            ]
        outs[k][pl.ds(AGG_ROW, ROWS - AGG_ROW), :] = agg[: ROWS - AGG_ROW]


def unpack_kernel(groups, *refs):
    ins, out_ref, stack = refs[:VECS], refs[VECS], refs[VECS + 1]
    own = lax.axis_index("gx") // groups
    count = BANDS * TX
    permute = (iota((CELLS, CELLS), 1) == source_lane(iota((CELLS, 1), 0))).astype(F32)
    for k in range(VECS):
        for t in range(TILES):
            stack[pl.ds(k * count, count), t * LANES : (t + 1) * LANES] = ins[k][
                pl.ds(t * count, count), :
            ]
    moved = sum(
        jnp.dot(part, permute.astype(BF16), preferred_element_type=F32) for part in split(stack[...])
    )
    for k in range(VECS):
        for b in range(BANDS):
            first = k * count + b * TX
            out_ref[own ^ k, b] = moved[first : first + TX]


def split(value):
    high = value.astype(BF16)
    left = value - high.astype(F32)
    middle = left.astype(BF16)
    return high, middle, (left - middle.astype(F32)).astype(BF16)


def order_kernel(source_ref, out_ref):
    size = NAGG * BANDS
    row, column = iota((size, 1), 0), iota((1, size), 1)
    inputs = (iota((size, size), 1) == (row % NAGG) * BANDS + row // NAGG).astype(F32).astype(BF16)
    outputs = (
        (iota((size, size), 0) == (column % NAGG) * BANDS + column // NAGG).astype(F32).astype(BF16)
    )
    turned = sum(
        lax.dot_general(inputs, part, (((1,), (1,)), ((), ())), preferred_element_type=F32)
        for part in split(source_ref[...])
    )
    ordered = jnp.dot(
        jnp.concatenate(split(turned), axis=0), outputs, preferred_element_type=F32
    )
    out_ref[...] = (ordered[:size] + ordered[size : 2 * size] + ordered[2 * size :]).reshape(
        BANDS, NAGG, size
    )


def solve_kernel(size_x, size_y, places, *refs):
    count = len(places)
    pieces, (coef, table, inverse_ref) = refs[:count], refs[count : count + 3]
    refs = refs[count - 1 :]
    outs = refs[4 : 4 + VECS]
    (
        scratch, basis, fresh, ext, work, pots, winv, sums, labels, aggs, onehot, pots_1, winv_1,
        pots_2, winv_2, sides, weights_f, weights, coupled, coupled_1, res_1, cor_1, res_2, cor_2, cells_2, kept, hess, scale, answer, arrived,
    ) = refs[4 + VECS :]
    groups = size_x // VECS
    lanes = size_y * GROUP
    plane = (size_x, lanes)
    halves = lanes // LANES
    my_x = lax.axis_index("gx")
    my_y = lax.axis_index("gy")
    own = my_x // groups
    my_g = my_x % groups

    sub = iota(plane, 0)
    lane = iota(plane, 1)
    first_x, last_x = sub == 0, sub == size_x - 1
    first_y, last_y = lane < ZQ, lane >= lanes - ZQ
    first_z, last_z = lane % ZQ == 0, lane % ZQ == ZQ - 1

    def shifted(value, amount, axis, mask):
        moved = pltpu.roll(value, amount % value.shape[axis], axis)
        return jnp.where(mask, 0.0, moved)

    def coupling(direction, a, b):
        return coef[direction, a, b]

    def centre(band):
        return 2.0 * (coupling(0, band, band) + coupling(1, band, band) + coupling(2, band, band))

    narrow = plane == (SUBLANES, LANES)
    copies = []
    for piece, blocks in zip(pieces, places):
        for i, (k, mask_g, mask_y) in enumerate(blocks):
            other_x, other_y = (own ^ k) * groups + (my_g ^ mask_g), my_y ^ mask_y
            if narrow:
                first = other_y * size_x + other_x
                scratch[pl.ds(first, ROWS, stride=size_x * size_y), :] = piece[i]
            else:
                target = scratch.at[:, other_y, other_x, :]
                copies.append(pltpu.make_async_copy(piece.at[i], target, arrived.at[len(copies)]))
    for copy in copies:
        copy.start()

    if narrow:
        row = iota((SUBLANES, PARTS), 0)
        column = iota((SUBLANES, PARTS), 1)
        band, part = (column // SUBLANES) % BANDS, column // (BANDS * SUBLANES)
        same = column % SUBLANES == row
        for a in range(BANDS):
            rows = [jnp.zeros((SUBLANES, PARTS), F32)] * 3
            for b in range(BANDS):
                rows = [jnp.where(band == b, coupling(d, a, b), rows[d]) for d in range(3)]
            rows = [2.0 * (rows[0] + rows[1] + rows[2])] + [-value for value in rows]
            for g, value in enumerate(rows):
                value = jnp.where(same, value, 0.0)
                high = value.astype(BF16).astype(F32)
                weights_f[pl.ds((g * BANDS + a) * SUBLANES, SUBLANES), :] = jnp.where(
                    part < 2, high, value - high
                )
        weights[...] = weights_f[...].astype(BF16)

    def mix(columns):
        parts = []
        for values in columns:
            value = jnp.concatenate(values, axis=0)
            high = value.astype(BF16)
            low = (value - high.astype(F32)).astype(BF16)
            parts.append(jnp.concatenate([high, low, high], axis=0))
        return jnp.dot(
            weights[...], jnp.concatenate(parts, axis=1), preferred_element_type=F32
        )

    def block_of(g, a, n):
        first = (g * BANDS + a) * SUBLANES
        return slice(first, first + SUBLANES), slice(n * LANES, (n + 1) * LANES)

    one_lane = iota((size_x, LANES), 1)
    low_64, low_32 = one_lane < 64, one_lane % 64 < 32

    def regroup(row):
        result = []
        for h in range(halves):
            if narrow:
                first = row * size_y * size_x
                g = [scratch[pl.ds(first + i * size_x, size_x), :] for i in range(4)]
            else:
                g = [scratch[row, 4 * h + i] for i in range(4)]
            for i in (0, 1):
                low, high = g[i], g[i + 2]
                g[i] = jnp.where(low_64, low, pltpu.roll(high, 64, 1))
                g[i + 2] = jnp.where(low_64, pltpu.roll(low, 64, 1), high)
            for i in (0, 2):
                low, high = g[i], g[i + 1]
                g[i] = jnp.where(low_32, low, pltpu.roll(high, 32, 1))
                g[i + 1] = jnp.where(low_32, pltpu.roll(low, 96, 1), high)
            result.append(g)
        return [
            result[0][c] if halves == 1 else jnp.concatenate([r[c] for r in result], axis=1)
            for c in range(4)
        ]

    def load_field(x, total):
        for t in range(TILES):
            for b in range(BANDS):
                for c, value in enumerate(regroup(t * BANDS * TX + b * TX + x)):
                    work[x, t * 4 + c, b] = value
                    for i in range(1, ITERS):
                        basis[i, x, t * 4 + c, b] = jnp.zeros(plane, F32)
                    total = total + value * value
            for c, value in enumerate(regroup(FIELD_ROWS + t * TX + x)):
                labels[x, t * 4 + c] = value
        return total

    for copy in copies:
        copy.wait()
    total = lax.fori_loop(0, TX, load_field, jnp.zeros(plane, F32))
    for k, value in enumerate(regroup(AGG_ROW)[:3]):
        aggs[k] = value

    def total_of(value):
        return jnp.broadcast_to(jnp.sum(value, keepdims=True), plane)

    for i in range((ITERS + 1) * ITERS):
        hess[i] = jnp.zeros(plane, F32)

    def fill(x, carry):
        for b in range(BANDS):
            diagonal = centre(b)
            for zt in range(ZT):
                for yt in range(YT):
                    label = labels[x, yt * ZT + zt]
                    value = jnp.zeros(plane, F32)
                    for r in range(REGIONS):
                        value = jnp.where(label == float(r), table[r, b], value)
                    pots[x, yt * ZT + zt, b] = value
                    winv[x, yt * ZT + zt, b] = OMEGA * (1.0 / (diagonal + value))
                    if zt % 2 == 0 and yt == 0:
                        four = value
                    else:
                        four = four + value
                if zt % 2 == 1:
                    sums[x, zt // 2, b] = four
        return carry

    lax.fori_loop(0, TX, fill, 0)

    even_z = lane % 2 == 0
    even_y = (lane // ZQ) % 2 == 0

    def restrict_2(q):
        near, far = q[0] + q[1], q[1] + q[2]
        p = [
            jnp.where(even_z, near, pltpu.roll(near, 1, 1)),
            jnp.where(even_z, q[2], q[0])
            + jnp.where(even_z, pltpu.roll(q[0], lanes - 1, 1), pltpu.roll(q[2], 1, 1)),
            jnp.where(even_z, pltpu.roll(far, lanes - 1, 1), far),
        ]
        return [
            0.125
            * (v + jnp.where(even_y, pltpu.roll(v, lanes - ZQ, 1), pltpu.roll(v, ZQ, 1)))
            for v in p
        ]

    for b in range(BANDS):
        q = []
        for z in range(3):
            pair = []
            for x in range(2):
                value = 0.125 * (sums[2 * x, z, b] + sums[2 * x + 1, z, b])
                pots_1[x, z, b] = value
                winv_1[x, z, b] = OMEGA * (1.0 / (0.25 * centre(b) + value))
                pair.append(value)
            q.append(pair[0] + pair[1])
        for k, value in enumerate(restrict_2(q)):
            pots_2[k, b] = value
            winv_2[k, b] = OMEGA * (1.0 / (0.0625 * centre(b) + value))

    for k in range(3):
        for h in range(halves):
            for x in range(size_x):
                n = (k * halves + h) * size_x + x
                row = aggs[k, x : x + 1, h * LANES : (h + 1) * LANES]
                onehot[:, n * LANES : (n + 1) * LANES] = (
                    (row == iota((NAGG, LANES), 0).astype(F32)).astype(F32).astype(BF16)
                )

    beta = jnp.sqrt(total_of(total))
    scale[...] = 1.0 / beta

    def ghosts():
        for c in range(COMBOS):
            for b in range(BANDS):
                if narrow:
                    rows, columns = block_of(1, b, c)
                    coupled[TX + 1, rows, columns] = shifted(coupled[1, rows, columns], -1, 0, last_x)
                    coupled[0, rows, columns] = shifted(coupled[TX, rows, columns], 1, 0, first_x)
                    continue
                ext[TX + 1, c, b] = shifted(ext[1, c, b], -1, 0, last_x)
                ext[0, c, b] = shifted(ext[TX, c, b], 1, 0, first_x)

    def combine(neighbours, count):
        acc = None
        for b in range(BANDS):
            differences = neighbours(b)
            new = []
            for a in range(BANDS):
                c = [coupling(d, a, b) for d in range(3)]
                row = []
                for n in range(count):
                    value = c[0] * differences[0][n]
                    value = value + c[1] * differences[1][n]
                    value = value + c[2] * differences[2][n]
                    row.append(value if acc is None else acc[a][n] + value)
                new.append(row)
            acc = new
        return acc

    def mix_some(x, c, row, columns):
        if not narrow:
            return
        columns.append(row)
        if len(columns) == 4:
            coupled[x + 1, :, (c - 3) * LANES : (c + 1) * LANES] = mix(columns)
            columns.clear()

    def mixed_0(x, cells):
        def at(g, a, yt, zt, dx=0):
            rows, columns = block_of(g, a, yt * ZT + zt)
            return coupled[x + 1 + dx, rows, columns]

        values = []
        for a in range(BANDS):
            row = []
            for yt, zt in cells:
                value = at(0, a, yt, zt) + (at(1, a, yt, zt, 1) + at(1, a, yt, zt, -1))
                partner = at(2, a, 1 - yt, zt)
                if yt == 0:
                    outer = shifted(partner, ZQ, 1, first_y)
                else:
                    outer = shifted(partner, -ZQ, 1, last_y)
                value = value + (partner + outer)
                if zt == 0:
                    below = shifted(at(3, a, yt, ZT - 1), 1, 1, first_z)
                else:
                    below = at(3, a, yt, zt - 1)
                if zt == ZT - 1:
                    above = shifted(at(3, a, yt, 0), -1, 1, last_z)
                else:
                    above = at(3, a, yt, zt + 1)
                value = value + (below + above)
                row.append(value + pots[x, yt * ZT + zt, a] * ext[x + 1, yt * ZT + zt, a])
            values.append(row)
        return values

    def mix_1(src):
        coupled_1[...] = mix([[src[x, z, b] for b in range(BANDS)] for x in range(2) for z in range(3)])

        def sides_of(d, a, x, z):
            def at(x, z):
                return coupled_1[block_of(d + 1, a, x * 3 + z)]

            mid = at(x, z)
            if d == 0:
                other = at(1 - x, z)
                if x == 0:
                    return mid, shifted(other, 1, 0, first_x), other
                return mid, other, shifted(other, -1, 0, last_x)
            if d == 1:
                return mid, shifted(mid, ZQ, 1, first_y), shifted(mid, -ZQ, 1, last_y)
            below = at(x, z - 1) if z > 0 else shifted(at(x, 2), 1, 1, first_z)
            above = at(x, z + 1) if z < 2 else shifted(at(x, 0), -1, 1, last_z)
            return mid, below, above

        return sides_of

    def operator_0(x, finish):
        for pair in range(ZT // 2):
            cells = [(yt, 2 * pair + i) for i in range(2) for yt in range(YT)]
            if narrow:
                finish(pair, cells, mixed_0(x, cells))
                continue

            def neighbours(b):
                def at(dx, yt, zt):
                    return ext[x + 1 + dx, yt * ZT + zt, b]

                mid = {cell: at(0, *cell) for cell in cells}
                along = [[], [], []]
                for yt, zt in cells:
                    twice = mid[yt, zt] + mid[yt, zt]
                    along[0].append(twice - (at(1, yt, zt) + at(-1, yt, zt)))
                    partner = mid[1 - yt, zt]
                    if yt == 0:
                        outer = shifted(partner, ZQ, 1, first_y)
                    else:
                        outer = shifted(partner, -ZQ, 1, last_y)
                    along[1].append(twice - (partner + outer))
                    if zt % 2 == 0:
                        inside = mid[yt, zt + 1]
                        if zt == 0:
                            outer = shifted(at(0, yt, ZT - 1), 1, 1, first_z)
                        else:
                            outer = at(0, yt, zt - 1)
                    else:
                        inside = mid[yt, zt - 1]
                        if zt == ZT - 1:
                            outer = shifted(at(0, yt, 0), -1, 1, last_z)
                        else:
                            outer = at(0, yt, zt + 1)
                    along[2].append(twice - (inside + outer))
                return along

            acc = combine(neighbours, len(cells))
            values = [
                [
                    acc[b][n] + pots[x, yt * ZT + zt, b] * ext[x + 1, yt * ZT + zt, b]
                    for n, (yt, zt) in enumerate(cells)
                ]
                for b in range(BANDS)
            ]
            finish(pair, cells, values)

    def operator_1(src, finish):
        for x in range(2):

            def neighbours(b):
                along = [[], [], []]
                mid = [src[x, z, b] for z in range(3)]
                for z in range(3):
                    twice = mid[z] + mid[z]
                    partner = src[1 - x, z, b]
                    if x == 0:
                        outer = shifted(partner, 1, 0, first_x)
                    else:
                        outer = shifted(partner, -1, 0, last_x)
                    along[0].append(twice - (partner + outer))
                    along[1].append(
                        twice
                        - (shifted(mid[z], ZQ, 1, first_y) + shifted(mid[z], -ZQ, 1, last_y))
                    )
                    below = mid[z - 1] if z > 0 else shifted(mid[2], 1, 1, first_z)
                    above = mid[z + 1] if z < 2 else shifted(mid[0], -1, 1, last_z)
                    along[2].append(twice - (below + above))
                return along

            acc = combine(neighbours, 3)
            finish(
                x,
                [
                    [0.25 * acc[b][z] + pots_1[x, z, b] * src[x, z, b] for z in range(3)]
                    for b in range(BANDS)
                ],
            )

    first_y2, last_y2 = lane < 2 * ZQ, lane >= lanes - 2 * ZQ
    first_z2, last_z2 = lane % ZQ < 2, lane % ZQ >= ZQ - 2

    def operator_2(src):
        def neighbours(b):
            along = [[], [], []]
            mid = [src[z, b] for z in range(3)]
            for z in range(3):
                twice = mid[z] + mid[z]
                along[0].append(
                    twice - (shifted(mid[z], 1, 0, first_x) + shifted(mid[z], -1, 0, last_x))
                )
                along[1].append(
                    twice
                    - (
                        shifted(mid[z], 2 * ZQ, 1, first_y2)
                        + shifted(mid[z], -2 * ZQ, 1, last_y2)
                    )
                )
                below = mid[z - 1] if z > 0 else shifted(mid[2], 2, 1, first_z2)
                above = mid[z + 1] if z < 2 else shifted(mid[0], -2, 1, last_z2)
                along[2].append(twice - (below + above))
            return along

        acc = combine(neighbours, 3)
        return [
            [0.0625 * acc[b][z] + pots_2[z, b] * src[z, b] for z in range(3)] for b in range(BANDS)
        ]

    single = even_y & even_z
    count_2 = 3 * halves * size_x

    def coarse(defect):
        for z in range(3):
            for b in range(8):
                if b < BANDS:
                    value = jnp.where(single, defect[b][z], 0.0)
                else:
                    value = jnp.zeros(plane, F32)
                for h in range(halves):
                    n = (z * halves + h) * size_x
                    cells_2[pl.ds(n * 8 + b, size_x, stride=8), :] = value[
                        :, h * LANES : (h + 1) * LANES
                    ]
        wide = jnp.concatenate(
            [cells_2[pl.ds(n * 8, 8), :] for n in range(count_2)], axis=1
        )
        partial = lax.dot_general(
            onehot[...],
            jnp.concatenate(split(wide), axis=0),
            (((1,), (1,)), ((), ())),
            preferred_element_type=F32,
        )
        partial = partial[:, :8] + partial[:, 8:16] + partial[:, 16:24]
        pairs = NAGG * BANDS // LANES
        acc = [jnp.zeros((8, LANES), F32)] * pairs
        for b in range(BANDS):
            column = jnp.broadcast_to(partial[:, b : b + 1], (NAGG, LANES))
            for i in range(NAGG // 8):
                for a in range(pairs):
                    acc[a] = (
                        acc[a]
                        + inverse_ref[b, pl.ds(i * 8, 8), a * LANES : (a + 1) * LANES]
                        * column[i * 8 : (i + 1) * 8]
                    )
        band = iota((8, LANES), 0)
        solved = jnp.zeros((8, LANES), F32)
        for a in range(pairs):
            both = jnp.broadcast_to(jnp.sum(acc[a], axis=0, keepdims=True), (8, LANES))
            solved = jnp.where(band == 2 * a, both, solved)
            solved = jnp.where(band == 2 * a + 1, pltpu.roll(both, NAGG, 1), solved)
        spread_out = jnp.dot(
            jnp.concatenate(split(solved[:, :NAGG]), axis=0), onehot[...], preferred_element_type=F32
        )
        spread_out = spread_out[:8] + spread_out[8:16] + spread_out[16:24]
        for n in range(count_2):
            cells_2[pl.ds(n * 8, 8), :] = spread_out[:, n * LANES : (n + 1) * LANES]

        def correction(b, z):
            parts = [
                cells_2[pl.ds(((z * halves + h) * size_x) * 8 + b, size_x, stride=8), :]
                for h in range(halves)
            ]
            return parts[0] if halves == 1 else jnp.concatenate(parts, axis=1)

        return correction

    def prolonged_sides():
        for x in range(2):
            for z in range(3):

                def neighbours(b):
                    mid = sums[x, z, b]
                    near_x = sums[1 - x, z, b]
                    if x == 0:
                        low_x, high_x = shifted(near_x, 1, 0, first_x), near_x
                    else:
                        low_x, high_x = near_x, shifted(near_x, -1, 0, last_x)
                    low_y, high_y = shifted(mid, ZQ, 1, first_y), shifted(mid, -ZQ, 1, last_y)
                    low_z = sums[x, z - 1, b] if z > 0 else shifted(sums[x, 2, b], 1, 1, first_z)
                    high_z = sums[x, z + 1, b] if z < 2 else shifted(sums[x, 0, b], -1, 1, last_z)
                    return [
                        [mid - low_x, mid - high_x],
                        [mid - low_y, mid - high_y],
                        [mid - low_z, mid - high_z],
                    ]

                acc = [None] * 3
                for b in range(BANDS):
                    differences = neighbours(b)
                    for d in range(3):
                        new = []
                        for a in range(BANDS):
                            c = coupling(d, a, b)
                            row = [c * value for value in differences[d]]
                            new.append(
                                row if b == 0 else [acc[d][a][i] + row[i] for i in range(2)]
                            )
                        acc[d] = new
                for d in range(3):
                    for side in range(2):
                        for a in range(BANDS):
                            sides[d, side, x, z, a] = acc[d][a][side]

    def over_x(body, carry):
        if not narrow:
            return lax.fori_loop(0, TX, body, carry)
        for x in range(TX):
            carry = body(x, carry)
        return carry

    def iteration(j, carry):
        factor = scale[...]

        def smooth(x, c_):
            columns = []
            for c in range(COMBOS):
                row = []
                for b in range(BANDS):
                    value = work[x, c, b] * factor
                    basis[j, x, c, b] = value
                    value = winv[x, c, b] * value
                    ext[x + 1, c, b] = value
                    row.append(value)
                mix_some(x, c, row, columns)
            return c_

        over_x(smooth, 0)
        ghosts()

        def down(x, c_):
            def finish(pair, cells, values):
                for b in range(BANDS):
                    defects = []
                    for n, (yt, zt) in enumerate(cells):
                        residual = basis[j, x, yt * ZT + zt, b]
                        defect = residual - values[b][n]
                        defects.append(defect)
                        work[x, yt * ZT + zt, b] = residual + defect
                    sums[x, pair, b] = (defects[0] + defects[1]) + (defects[2] + defects[3])

            operator_0(x, finish)
            return c_

        over_x(down, 0)

        for x in range(2):
            for z in range(3):
                for b in range(BANDS):
                    value = 0.125 * (sums[2 * x, z, b] + sums[2 * x + 1, z, b])
                    res_1[x, z, b] = value
                    cor_1[x, z, b] = winv_1[x, z, b] * value

        def defect_1(x, values):
            for b in range(BANDS):
                for z in range(3):
                    value = res_1[x, z, b] - values[b][z]
                    if x == 0:
                        sums[0, z, b] = value
                    else:
                        sums[0, z, b] = sums[0, z, b] + value

        operator_1(cor_1, defect_1)
        for b in range(BANDS):
            for z, value in enumerate(restrict_2([sums[0, z, b] for z in range(3)])):
                res_2[z, b] = value
                cor_2[z, b] = winv_2[z, b] * value
        values = operator_2(cor_2)
        correction = coarse(
            [[res_2[z, b] - values[b][z] for z in range(3)] for b in range(BANDS)]
        )
        for b in range(BANDS):
            for z in range(3):
                cor_2[z, b] = cor_2[z, b] + correction(b, z)
        values = operator_2(cor_2)
        for b in range(BANDS):
            e = [
                cor_2[z, b] + winv_2[z, b] * (res_2[z, b] - values[b][z]) for z in range(3)
            ]
            fine = [
                jnp.where(even_z, e[0], e[1]),
                jnp.where(even_z, e[0], e[2]),
                jnp.where(even_z, e[1], e[2]),
            ]
            for x in range(2):
                for z in range(3):
                    cor_1[x, z, b] = cor_1[x, z, b] + fine[z]

        def post_1(x, values):
            for b in range(BANDS):
                for z in range(3):
                    sums[x, z, b] = cor_1[x, z, b] + winv_1[x, z, b] * (
                        res_1[x, z, b] - values[b][z]
                    )

        operator_1(cor_1, post_1)

        if narrow:
            sides_of = mix_1(sums)
            for d in range(3):
                for x in range(2):
                    for z in range(3):
                        for a in range(BANDS):
                            mid, low, high = sides_of(d, a, x, z)
                            sides[d, 0, x, z, a] = low - mid
                            sides[d, 1, x, z, a] = high - mid
        else:
            prolonged_sides()

        def up(x, c_):
            columns = []
            for yt in range(YT):
                for zt in range(ZT):
                    z, c = zt // 2, yt * ZT + zt
                    row = []
                    for b in range(BANDS):
                        coarse_value = sums[x // 2, z, b]
                        applied = (
                            (sides[0, x % 2, x // 2, z, b] + sides[1, yt, x // 2, z, b])
                            + sides[2, zt % 2, x // 2, z, b]
                            + pots[x, c, b] * coarse_value
                        )
                        value = coarse_value + winv[x, c, b] * (work[x, c, b] - applied)
                        ext[x + 1, c, b] = value
                        row.append(value)
                    mix_some(x, c, row, columns)
            return c_

        over_x(up, 0)
        ghosts()

        def apply(x, parts):
            parts = list(parts)

            def finish(pair, cells, values):
                for b in range(BANDS):
                    for n, (yt, zt) in enumerate(cells):
                        c = yt * ZT + zt
                        fresh[x, c, b] = values[b][n]
                        for i in range(ITERS):
                            parts[i] = parts[i] + basis[i, x, c, b] * values[b][n]

            operator_0(x, finish)
            quarter = one_lane // GROUP
            for b in range(BANDS):
                for t in range(TILES):
                    merged = None
                    for i in range(4):
                        moved = pltpu.roll(
                            ext[x + 1, t * 4 + i, b], (GROUP * i + lanes - GROUP * my_y) % lanes, 1
                        )[:, :LANES]
                        merged = moved if i == 0 else jnp.where(quarter == i, moved, merged)
                    kept[j, x, b * TILES + t] = merged
            return tuple(parts)

        parts = over_x(apply, (jnp.zeros(plane, F32),) * ITERS)
        projections = [total_of(part) for part in parts]
        for i in range(ITERS):
            hess[i * ITERS + j] = projections[i]

        def subtract(x, parts):
            parts = list(parts)
            for c in range(COMBOS):
                for b in range(BANDS):
                    n = (c * BANDS + b) % 4
                    value = fresh[x, c, b]
                    for i in range(ITERS):
                        value = value - projections[i] * basis[i, x, c, b]
                    work[x, c, b] = value
                    parts[n] = parts[n] + value * value
            return tuple(parts)

        parts = lax.fori_loop(0, TX, subtract, (jnp.zeros(plane, F32),) * 4)
        total = (parts[0] + parts[1]) + (parts[2] + parts[3])
        norm = jnp.sqrt(total_of(total))
        hess[(j + 1) * ITERS + j] = norm
        scale[...] = 1.0 / norm
        return carry

    lax.fori_loop(0, ITERS, iteration, 0)

    h = [[hess[i * ITERS + j][:, :LANES] for j in range(ITERS)] for i in range(ITERS + 1)]
    normal = [
        [sum(h[i][j] * h[i][k] for i in range(ITERS + 1)) for k in range(ITERS)]
        for j in range(ITERS)
    ]
    first = beta[:, :LANES]
    weights = solve_small(normal, [first * h[0][j] for j in range(ITERS)], ITERS)

    for x in range(TX):
        for b in range(BANDS):
            for t in range(TILES):
                value = weights[0] * kept[0, x, b * TILES + t]
                for j in range(1, ITERS):
                    value = value + weights[j] * kept[j, x, b * TILES + t]
                value = pltpu.roll(value, (size_x - my_g) % size_x, 0)
                row = t * BANDS * TX + b * TX + x
                for z in range(VECS):
                    answer[z, row : row + 1, :] = value[z * groups : z * groups + 1]
    for k in range(VECS):
        outs[k][...] = answer[own ^ k]


def solve_small(normal_matrix, right_side, count):
    factor = {}
    for i in range(count):
        for k in range(i + 1):
            running = normal_matrix[i][k]
            for m in range(k):
                running = running - factor[i, m] * factor[k, m]
            if i == k:
                factor[i, i] = jnp.sqrt(running)
            else:
                factor[i, k] = running / factor[k, k]
    forward = []
    for i in range(count):
        running = right_side[i]
        for k in range(i):
            running = running - factor[i, k] * forward[k]
        forward.append(running / factor[i, i])
    answer = [None] * count
    for i in reversed(range(count)):
        running = forward[i]
        for k in range(i + 1, count):
            running = running - factor[k, i] * answer[k]
        answer[i] = running / factor[i, i]
    return answer


VMEM_SPEC = pl.BlockSpec(memory_space=pltpu.VMEM)
HBM_SPEC = pl.BlockSpec(memory_space=pltpu.HBM)
ANY_SPEC = pl.BlockSpec(memory_space=pl.ANY)
SMEM_SPEC = pl.BlockSpec(memory_space=pltpu.SMEM)


def bits(count):
    return count.bit_length() - 1


def shards(
    size_x, size_y, right_hand, region_labels, potential_table, coupling, aggregate_map,
    coarse_inverse,
):
    groups = size_x // VECS
    devices = size_x * size_y
    names = ("gx", "gy")
    stride = groups * size_y

    def exchanged(value, mask):
        return lax.ppermute(value, names, [(i, i ^ mask) for i in range(devices)])

    row_shape = jax.ShapeDtypeStruct((ROWS, LANES), F32)
    count = BANDS * TX
    packed = pl.pallas_call(
        functools.partial(pack_kernel, groups),
        out_shape=[row_shape] * VECS,
        in_specs=[HBM_SPEC] * 3,
        out_specs=[VMEM_SPEC] * VECS,
        scratch_shapes=[
            pltpu.VMEM((VECS * count + 8, CELLS), F32),
            pltpu.VMEM(right_hand.shape, F32),
            pltpu.VMEM(region_labels.shape, jnp.int32),
            pltpu.VMEM(aggregate_map.shape, jnp.int32),
            pltpu.SemaphoreType.DMA((3,)),
        ],
        compiler_params=pltpu.CompilerParams(vmem_limit_bytes=60 * 2**20),
        name="pack",
    )(right_hand, region_labels, aggregate_map)
    packed, coarse_inverse = lax.optimization_barrier((packed, coarse_inverse))
    turns = (0, 2, 3, 1)
    parts = [packed[0]] + [exchanged(packed[k], k * stride) for k in turns[1:]]
    inverse = pl.pallas_call(
        order_kernel,
        out_shape=jax.ShapeDtypeStruct((BANDS, NAGG, BANDS * NAGG), F32),
        in_specs=[VMEM_SPEC],
        out_specs=VMEM_SPEC,
        compiler_params=pltpu.CompilerParams(vmem_limit_bytes=16 * 2**20),
        cost_estimate=pl.CostEstimate(
            flops=6 * (NAGG * BANDS) ** 3, bytes_accessed=2**21, transcendentals=0
        ),
        name="order",
    )(coarse_inverse)

    steps = [("gy", i) for i in range(bits(size_y) - 1, 0, -1)]
    steps += [("gx", i) for i in range(bits(groups))]
    second, inverse = lax.optimization_barrier((jnp.stack(parts[2:]), inverse))
    halves = [[jnp.stack(parts[:2])], [second]]
    places = [[[(k, 0, 0) for k in turns[:2]]], [[(k, 0, 0) for k in turns[2:]]]]

    def widen(half, axis, bit):
        mask = 1 << bit
        sent = halves[half][0] if len(halves[half]) == 1 else jnp.concatenate(halves[half])
        halves[half].append(exchanged(sent, mask * (size_y if axis == "gx" else 1)))
        mask_g, mask_y = (mask, 0) if axis == "gx" else (0, mask)
        places[half].append(
            [(k, g ^ mask_g, y ^ mask_y) for blocks in places[half] for k, g, y in blocks]
        )

    for first, last in zip(steps, steps):
        widen(0, *first)
        widen(1, *last)
    widen(0, "gy", 0)
    widen(1, "gy", 0)
    pieces = halves[0] + halves[1]
    places = places[0] + places[1]

    lanes = size_y * GROUP
    plane = (size_x, lanes)
    count_2 = 3 * (lanes // LANES) * size_x
    narrow = plane == (SUBLANES, LANES)
    vmem = lambda *shape: pltpu.VMEM(shape + plane, F32)
    scratch = [
        pltpu.VMEM((ROWS * devices, LANES) if narrow else (ROWS, size_y, size_x, LANES), F32),
        vmem(ITERS, TX, COMBOS, BANDS),
        vmem(TX, COMBOS, BANDS),
        vmem(TX + 2, COMBOS, BANDS),
        vmem(TX, COMBOS, BANDS),
        vmem(TX, COMBOS, BANDS),
        vmem(TX, COMBOS, BANDS),
        vmem(TX, 3, BANDS),
        vmem(TX, COMBOS),
        vmem(3),
        pltpu.VMEM((NAGG, count_2 * LANES), BF16),
        vmem(2, 3, BANDS),
        vmem(2, 3, BANDS),
        vmem(3, BANDS),
        vmem(3, BANDS),
        vmem(3, 2, 2, 3, BANDS),
        pltpu.VMEM((MIXED, PARTS), F32),
        pltpu.VMEM((MIXED, PARTS), BF16),
        pltpu.VMEM((TX + 2, MIXED, COMBOS * LANES) if narrow else (8, LANES), F32),
        pltpu.VMEM((MIXED, 2 * TILES * LANES), F32),
        vmem(2, 3, BANDS),
        vmem(2, 3, BANDS),
        vmem(3, BANDS),
        vmem(3, BANDS),
        pltpu.VMEM((count_2 * 8, LANES), F32),
        pltpu.VMEM((ITERS, TX, BANDS * TILES, size_x, LANES), F32),
        vmem((ITERS + 1) * ITERS),
        vmem(),
        pltpu.VMEM((VECS, FIELD_ROWS, LANES), F32),
        pltpu.SemaphoreType.DMA((devices,)),
    ]
    held = sum(math.prod(ref.shape) * 4 for ref in scratch)
    answers = pl.pallas_call(
        functools.partial(solve_kernel, size_x, size_y, places),
        out_shape=[jax.ShapeDtypeStruct((FIELD_ROWS, LANES), F32)] * VECS,
        in_specs=[VMEM_SPEC if narrow else ANY_SPEC] * len(pieces) + [SMEM_SPEC, SMEM_SPEC, VMEM_SPEC],
        out_specs=[VMEM_SPEC] * VECS,
        scratch_shapes=scratch,
        compiler_params=pltpu.CompilerParams(
            vmem_limit_bytes=min(held + 6 * 2**20, 63 * 2**20)
        ),
        name="solve",
    )(*pieces, coupling, potential_table, inverse)
    received = [answers[0]] + [exchanged(answers[k], k * stride) for k in range(1, VECS)]
    return pl.pallas_call(
        functools.partial(unpack_kernel, groups),
        out_shape=jax.ShapeDtypeStruct(right_hand.shape, F32),
        in_specs=[VMEM_SPEC] * VECS,
        out_specs=VMEM_SPEC,
        scratch_shapes=[pltpu.VMEM((VECS * count, CELLS), F32)],
        compiler_params=pltpu.CompilerParams(vmem_limit_bytes=8 * 2**20),
        name="unpack",
    )(*received)


def solution(mesh):
    return jax.shard_map(
        functools.partial(shards, mesh.shape["gx"], mesh.shape["gy"]),
        mesh=mesh,
        in_specs=(P(None, None, "gx", "gy"), P("gx", "gy"), P(), P(), P("gx", "gy"), P()),
        out_specs=P(None, None, "gx", "gy"),
        check_vma=False,
    )
```

```python
import functools
import math

import jax
import jax.numpy as jnp
from jax import lax
from jax.experimental import pallas as pl
from jax.experimental.pallas import tpu as pltpu
from jax.sharding import PartitionSpec as P

NZ = 48
BANDS = 6
VECS = 4
REGIONS = 3
ITERS = 3
NAGG = 64
OMEGA = 0.7

HIGHEST = lax.Precision.HIGHEST
F32 = jnp.float32
BF16 = jnp.bfloat16

TX = 4
TY = 8
YT = 2
ZT = 6
COMBOS = YT * ZT
ZQ = NZ // ZT
GROUP = (TY // YT) * ZQ
TILES = 3
FIELD_ROWS = TILES * BANDS * TX
LABEL_ROWS = TILES * TX
AGG_ROW = FIELD_ROWS + LABEL_ROWS
ROWS = 88
LANES = 128
CELLS = TY * NZ
SUBLANES = 8
MIXED = 4 * BANDS * SUBLANES
PARTS = 3 * BANDS * SUBLANES


def source_lane(target):
    combo = target // GROUP
    rest = target % GROUP
    return ((rest // ZQ) * YT + combo // ZT) * NZ + (rest % ZQ) * ZT + combo % ZT


def iota(shape, dim):
    return lax.broadcasted_iota(jnp.int32, shape, dim)


def pack_kernel(groups, right_hbm, labels_hbm, agg_hbm, *rest):
    outs, (stack, right_ref, labels_ref, agg_ref, arrived) = rest[:VECS], rest[VECS:]
    own = lax.axis_index("gx") // groups
    copies = [
        pltpu.make_async_copy(source, target, arrived.at[i])
        for i, (source, target) in enumerate(
            ((right_hbm, right_ref), (labels_hbm, labels_ref), (agg_hbm, agg_ref))
        )
    ]
    for copy in copies:
        copy.start()
    permute = (iota((CELLS, CELLS), 0) == source_lane(iota((1, CELLS), 1))).astype(F32)
    count = BANDS * TX
    for copy in copies:
        copy.wait()
    for k in range(VECS):
        for b in range(BANDS):
            stack[pl.ds(k * count + b * TX, TX), :] = right_ref[own ^ k, b]
    stack[pl.ds(VECS * count, TX), :] = labels_ref[...].astype(F32)
    stack[pl.ds(VECS * count + TX, TX), :] = jnp.zeros((TX, CELLS), F32)
    moved = sum(
        jnp.dot(part, permute.astype(BF16), preferred_element_type=F32) for part in split(stack[...])
    )
    lane = iota((1, LANES), 1)
    inner = lane % GROUP
    wanted = (inner // (2 * ZQ)) * (NZ // 4) + 3 * ((inner % ZQ) // 2) + lane // GROUP
    wanted = jnp.where(lane < 3 * GROUP, wanted, -1)
    cells = agg_ref.shape[1]
    pick = (iota((cells, LANES), 0) == wanted).astype(F32)
    agg = jnp.dot(
        jnp.broadcast_to(agg_ref[...].astype(F32), (8, cells)),
        pick,
        precision=HIGHEST,
        preferred_element_type=F32,
    )
    for k in range(VECS):
        for t in range(TILES):
            tile = slice(t * LANES, (t + 1) * LANES)
            outs[k][pl.ds(t * count, count), :] = moved[k * count : (k + 1) * count, tile]
            outs[k][pl.ds(FIELD_ROWS + t * TX, TX), :] = moved[
                VECS * count : VECS * count + TX, tile
            ]
        outs[k][pl.ds(AGG_ROW, ROWS - AGG_ROW), :] = agg[: ROWS - AGG_ROW]


def unpack_kernel(groups, *refs):
    ins, (permute_ref, out_ref, stack) = refs[:VECS], refs[VECS:]
    own = lax.axis_index("gx") // groups
    count = BANDS * TX
    for k in range(VECS):
        for t in range(TILES):
            stack[pl.ds(k * count, count), t * LANES : (t + 1) * LANES] = ins[k][
                pl.ds(t * count, count), :
            ]
    moved = sum(
        jnp.dot(part, permute_ref[...], preferred_element_type=F32) for part in split(stack[...])
    )
    for k in range(VECS):
        for b in range(BANDS):
            first = k * count + b * TX
            out_ref[own ^ k, b] = moved[first : first + TX]


def split(value):
    high = value.astype(BF16)
    left = value - high.astype(F32)
    middle = left.astype(BF16)
    return high, middle, (left - middle.astype(F32)).astype(BF16)


def order_kernel(source_ref, out_ref, permute_ref):
    permute_ref[...] = (
        (iota((CELLS, CELLS), 1) == source_lane(iota((CELLS, 1), 0))).astype(F32).astype(BF16)
    )
    size = NAGG * BANDS
    row, column = iota((size, 1), 0), iota((1, size), 1)
    inputs = (iota((size, size), 1) == (row % NAGG) * BANDS + row // NAGG).astype(F32).astype(BF16)
    outputs = (
        (iota((size, size), 0) == (column % NAGG) * BANDS + column // NAGG).astype(F32).astype(BF16)
    )
    turned = sum(
        lax.dot_general(inputs, part, (((1,), (1,)), ((), ())), preferred_element_type=F32)
        for part in split(source_ref[...])
    )
    ordered = jnp.dot(
        jnp.concatenate(split(turned), axis=0), outputs, preferred_element_type=F32
    )
    out_ref[...] = (ordered[:size] + ordered[size : 2 * size] + ordered[2 * size :]).reshape(
        BANDS, NAGG, size
    )


def solve_kernel(size_x, size_y, places, *refs):
    count = len(places)
    pieces, (coef, table, inverse_ref) = refs[:count], refs[count : count + 3]
    refs = refs[count - 1 :]
    outs = refs[4 : 4 + VECS]
    (
        scratch, basis, fresh, ext, work, pots, winv, sums, labels, aggs, onehot, pots_1, winv_1,
        pots_2, winv_2, sides, weights_f, weights, coupled, coupled_1, res_1, cor_1, res_2, cor_2, cells_2, kept, hess, scale, answer, arrived,
    ) = refs[4 + VECS :]
    groups = size_x // VECS
    lanes = size_y * GROUP
    plane = (size_x, lanes)
    halves = lanes // LANES
    my_x = lax.axis_index("gx")
    my_y = lax.axis_index("gy")
    own = my_x // groups
    my_g = my_x % groups

    sub = iota(plane, 0)
    lane = iota(plane, 1)
    first_x, last_x = sub == 0, sub == size_x - 1
    first_y, last_y = lane < ZQ, lane >= lanes - ZQ
    first_z, last_z = lane % ZQ == 0, lane % ZQ == ZQ - 1

    def shifted(value, amount, axis, mask):
        moved = pltpu.roll(value, amount % value.shape[axis], axis)
        return jnp.where(mask, 0.0, moved)

    def coupling(direction, a, b):
        return coef[direction, a, b]

    def centre(band):
        return 2.0 * (coupling(0, band, band) + coupling(1, band, band) + coupling(2, band, band))

    narrow = plane == (SUBLANES, LANES)
    copies = []
    for piece, blocks in zip(pieces, places):
        for i, (k, mask_g, mask_y) in enumerate(blocks):
            other_x, other_y = (own ^ k) * groups + (my_g ^ mask_g), my_y ^ mask_y
            if narrow:
                first = other_y * size_x + other_x
                scratch[pl.ds(first, ROWS, stride=size_x * size_y), :] = piece[i]
            else:
                target = scratch.at[:, other_y, other_x, :]
                copies.append(pltpu.make_async_copy(piece.at[i], target, arrived.at[len(copies)]))
    for copy in copies:
        copy.start()

    if narrow:
        row = iota((SUBLANES, PARTS), 0)
        column = iota((SUBLANES, PARTS), 1)
        band, part = (column // SUBLANES) % BANDS, column // (BANDS * SUBLANES)
        same = column % SUBLANES == row
        for a in range(BANDS):
            rows = [jnp.zeros((SUBLANES, PARTS), F32)] * 3
            for b in range(BANDS):
                rows = [jnp.where(band == b, coupling(d, a, b), rows[d]) for d in range(3)]
            rows = [2.0 * (rows[0] + rows[1] + rows[2])] + [-value for value in rows]
            for g, value in enumerate(rows):
                value = jnp.where(same, value, 0.0)
                high = value.astype(BF16).astype(F32)
                weights_f[pl.ds((g * BANDS + a) * SUBLANES, SUBLANES), :] = jnp.where(
                    part < 2, high, value - high
                )
        weights[...] = weights_f[...].astype(BF16)

    def mix(columns):
        parts = []
        for values in columns:
            value = jnp.concatenate(values, axis=0)
            high = value.astype(BF16)
            low = (value - high.astype(F32)).astype(BF16)
            parts.append(jnp.concatenate([high, low, high], axis=0))
        return jnp.dot(
            weights[...], jnp.concatenate(parts, axis=1), preferred_element_type=F32
        )

    def block_of(g, a, n):
        first = (g * BANDS + a) * SUBLANES
        return slice(first, first + SUBLANES), slice(n * LANES, (n + 1) * LANES)

    one_lane = iota((size_x, LANES), 1)
    low_64, low_32 = one_lane < 64, one_lane % 64 < 32

    def regroup(row):
        result = []
        for h in range(halves):
            if narrow:
                first = row * size_y * size_x
                g = [scratch[pl.ds(first + i * size_x, size_x), :] for i in range(4)]
            else:
                g = [scratch[row, 4 * h + i] for i in range(4)]
            for i in (0, 1):
                low, high = g[i], g[i + 2]
                g[i] = jnp.where(low_64, low, pltpu.roll(high, 64, 1))
                g[i + 2] = jnp.where(low_64, pltpu.roll(low, 64, 1), high)
            for i in (0, 2):
                low, high = g[i], g[i + 1]
                g[i] = jnp.where(low_32, low, pltpu.roll(high, 32, 1))
                g[i + 1] = jnp.where(low_32, pltpu.roll(low, 96, 1), high)
            result.append(g)
        return [
            result[0][c] if halves == 1 else jnp.concatenate([r[c] for r in result], axis=1)
            for c in range(4)
        ]

    def load_field(x, total):
        for t in range(TILES):
            for b in range(BANDS):
                for c, value in enumerate(regroup(t * BANDS * TX + b * TX + x)):
                    work[x, t * 4 + c, b] = value
                    for i in range(1, ITERS):
                        basis[i, x, t * 4 + c, b] = jnp.zeros(plane, F32)
                    total = total + value * value
            for c, value in enumerate(regroup(FIELD_ROWS + t * TX + x)):
                labels[x, t * 4 + c] = value
        return total

    for copy in copies:
        copy.wait()
    total = lax.fori_loop(0, TX, load_field, jnp.zeros(plane, F32))
    for k, value in enumerate(regroup(AGG_ROW)[:3]):
        aggs[k] = value

    def total_of(value):
        return jnp.broadcast_to(jnp.sum(value, keepdims=True), plane)

    for i in range((ITERS + 1) * ITERS):
        hess[i] = jnp.zeros(plane, F32)

    def fill(x, carry):
        for b in range(BANDS):
            diagonal = centre(b)
            for zt in range(ZT):
                for yt in range(YT):
                    label = labels[x, yt * ZT + zt]
                    value = jnp.zeros(plane, F32)
                    for r in range(REGIONS):
                        value = jnp.where(label == float(r), table[r, b], value)
                    pots[x, yt * ZT + zt, b] = value
                    winv[x, yt * ZT + zt, b] = OMEGA * (1.0 / (diagonal + value))
                    if zt % 2 == 0 and yt == 0:
                        four = value
                    else:
                        four = four + value
                if zt % 2 == 1:
                    sums[x, zt // 2, b] = four
        return carry

    lax.fori_loop(0, TX, fill, 0)

    even_z = lane % 2 == 0
    even_y = (lane // ZQ) % 2 == 0

    def restrict_2(q):
        near, far = q[0] + q[1], q[1] + q[2]
        p = [
            jnp.where(even_z, near, pltpu.roll(near, 1, 1)),
            jnp.where(even_z, q[2], q[0])
            + jnp.where(even_z, pltpu.roll(q[0], lanes - 1, 1), pltpu.roll(q[2], 1, 1)),
            jnp.where(even_z, pltpu.roll(far, lanes - 1, 1), far),
        ]
        return [
            0.125
            * (v + jnp.where(even_y, pltpu.roll(v, lanes - ZQ, 1), pltpu.roll(v, ZQ, 1)))
            for v in p
        ]

    for b in range(BANDS):
        q = []
        for z in range(3):
            pair = []
            for x in range(2):
                value = 0.125 * (sums[2 * x, z, b] + sums[2 * x + 1, z, b])
                pots_1[x, z, b] = value
                winv_1[x, z, b] = OMEGA * (1.0 / (0.25 * centre(b) + value))
                pair.append(value)
            q.append(pair[0] + pair[1])
        for k, value in enumerate(restrict_2(q)):
            pots_2[k, b] = value
            winv_2[k, b] = OMEGA * (1.0 / (0.0625 * centre(b) + value))

    for k in range(3):
        for h in range(halves):
            for x in range(size_x):
                n = (k * halves + h) * size_x + x
                row = aggs[k, x : x + 1, h * LANES : (h + 1) * LANES]
                onehot[:, n * LANES : (n + 1) * LANES] = (
                    (row == iota((NAGG, LANES), 0).astype(F32)).astype(F32).astype(BF16)
                )

    beta = jnp.sqrt(total_of(total))
    scale[...] = 1.0 / beta

    def ghosts():
        for c in range(COMBOS):
            for b in range(BANDS):
                if narrow:
                    rows, columns = block_of(1, b, c)
                    coupled[TX + 1, rows, columns] = shifted(coupled[1, rows, columns], -1, 0, last_x)
                    coupled[0, rows, columns] = shifted(coupled[TX, rows, columns], 1, 0, first_x)
                    continue
                ext[TX + 1, c, b] = shifted(ext[1, c, b], -1, 0, last_x)
                ext[0, c, b] = shifted(ext[TX, c, b], 1, 0, first_x)

    def combine(neighbours, count):
        acc = None
        for b in range(BANDS):
            differences = neighbours(b)
            new = []
            for a in range(BANDS):
                c = [coupling(d, a, b) for d in range(3)]
                row = []
                for n in range(count):
                    value = c[0] * differences[0][n]
                    value = value + c[1] * differences[1][n]
                    value = value + c[2] * differences[2][n]
                    row.append(value if acc is None else acc[a][n] + value)
                new.append(row)
            acc = new
        return acc

    def mix_some(x, c, row, columns):
        if not narrow:
            return
        columns.append(row)
        if len(columns) == 4:
            coupled[x + 1, :, (c - 3) * LANES : (c + 1) * LANES] = mix(columns)
            columns.clear()

    def mixed_0(x, cells):
        def at(g, a, yt, zt, dx=0):
            rows, columns = block_of(g, a, yt * ZT + zt)
            return coupled[x + 1 + dx, rows, columns]

        values = []
        for a in range(BANDS):
            row = []
            for yt, zt in cells:
                value = at(0, a, yt, zt) + (at(1, a, yt, zt, 1) + at(1, a, yt, zt, -1))
                partner = at(2, a, 1 - yt, zt)
                if yt == 0:
                    outer = shifted(partner, ZQ, 1, first_y)
                else:
                    outer = shifted(partner, -ZQ, 1, last_y)
                value = value + (partner + outer)
                if zt == 0:
                    below = shifted(at(3, a, yt, ZT - 1), 1, 1, first_z)
                else:
                    below = at(3, a, yt, zt - 1)
                if zt == ZT - 1:
                    above = shifted(at(3, a, yt, 0), -1, 1, last_z)
                else:
                    above = at(3, a, yt, zt + 1)
                value = value + (below + above)
                row.append(value + pots[x, yt * ZT + zt, a] * ext[x + 1, yt * ZT + zt, a])
            values.append(row)
        return values

    def mix_1(src):
        coupled_1[...] = mix([[src[x, z, b] for b in range(BANDS)] for x in range(2) for z in range(3)])

        def sides_of(d, a, x, z):
            def at(x, z):
                return coupled_1[block_of(d + 1, a, x * 3 + z)]

            mid = at(x, z)
            if d == 0:
                other = at(1 - x, z)
                if x == 0:
                    return mid, shifted(other, 1, 0, first_x), other
                return mid, other, shifted(other, -1, 0, last_x)
            if d == 1:
                return mid, shifted(mid, ZQ, 1, first_y), shifted(mid, -ZQ, 1, last_y)
            below = at(x, z - 1) if z > 0 else shifted(at(x, 2), 1, 1, first_z)
            above = at(x, z + 1) if z < 2 else shifted(at(x, 0), -1, 1, last_z)
            return mid, below, above

        return sides_of

    def operator_0(x, finish):
        for pair in range(ZT // 2):
            cells = [(yt, 2 * pair + i) for i in range(2) for yt in range(YT)]
            if narrow:
                finish(pair, cells, mixed_0(x, cells))
                continue

            def neighbours(b):
                def at(dx, yt, zt):
                    return ext[x + 1 + dx, yt * ZT + zt, b]

                mid = {cell: at(0, *cell) for cell in cells}
                along = [[], [], []]
                for yt, zt in cells:
                    twice = mid[yt, zt] + mid[yt, zt]
                    along[0].append(twice - (at(1, yt, zt) + at(-1, yt, zt)))
                    partner = mid[1 - yt, zt]
                    if yt == 0:
                        outer = shifted(partner, ZQ, 1, first_y)
                    else:
                        outer = shifted(partner, -ZQ, 1, last_y)
                    along[1].append(twice - (partner + outer))
                    if zt % 2 == 0:
                        inside = mid[yt, zt + 1]
                        if zt == 0:
                            outer = shifted(at(0, yt, ZT - 1), 1, 1, first_z)
                        else:
                            outer = at(0, yt, zt - 1)
                    else:
                        inside = mid[yt, zt - 1]
                        if zt == ZT - 1:
                            outer = shifted(at(0, yt, 0), -1, 1, last_z)
                        else:
                            outer = at(0, yt, zt + 1)
                    along[2].append(twice - (inside + outer))
                return along

            acc = combine(neighbours, len(cells))
            values = [
                [
                    acc[b][n] + pots[x, yt * ZT + zt, b] * ext[x + 1, yt * ZT + zt, b]
                    for n, (yt, zt) in enumerate(cells)
                ]
                for b in range(BANDS)
            ]
            finish(pair, cells, values)

    def operator_1(src, finish):
        for x in range(2):

            def neighbours(b):
                along = [[], [], []]
                mid = [src[x, z, b] for z in range(3)]
                for z in range(3):
                    twice = mid[z] + mid[z]
                    partner = src[1 - x, z, b]
                    if x == 0:
                        outer = shifted(partner, 1, 0, first_x)
                    else:
                        outer = shifted(partner, -1, 0, last_x)
                    along[0].append(twice - (partner + outer))
                    along[1].append(
                        twice
                        - (shifted(mid[z], ZQ, 1, first_y) + shifted(mid[z], -ZQ, 1, last_y))
                    )
                    below = mid[z - 1] if z > 0 else shifted(mid[2], 1, 1, first_z)
                    above = mid[z + 1] if z < 2 else shifted(mid[0], -1, 1, last_z)
                    along[2].append(twice - (below + above))
                return along

            acc = combine(neighbours, 3)
            finish(
                x,
                [
                    [0.25 * acc[b][z] + pots_1[x, z, b] * src[x, z, b] for z in range(3)]
                    for b in range(BANDS)
                ],
            )

    first_y2, last_y2 = lane < 2 * ZQ, lane >= lanes - 2 * ZQ
    first_z2, last_z2 = lane % ZQ < 2, lane % ZQ >= ZQ - 2

    def operator_2(src):
        def neighbours(b):
            along = [[], [], []]
            mid = [src[z, b] for z in range(3)]
            for z in range(3):
                twice = mid[z] + mid[z]
                along[0].append(
                    twice - (shifted(mid[z], 1, 0, first_x) + shifted(mid[z], -1, 0, last_x))
                )
                along[1].append(
                    twice
                    - (
                        shifted(mid[z], 2 * ZQ, 1, first_y2)
                        + shifted(mid[z], -2 * ZQ, 1, last_y2)
                    )
                )
                below = mid[z - 1] if z > 0 else shifted(mid[2], 2, 1, first_z2)
                above = mid[z + 1] if z < 2 else shifted(mid[0], -2, 1, last_z2)
                along[2].append(twice - (below + above))
            return along

        acc = combine(neighbours, 3)
        return [
            [0.0625 * acc[b][z] + pots_2[z, b] * src[z, b] for z in range(3)] for b in range(BANDS)
        ]

    single = even_y & even_z
    count_2 = 3 * halves * size_x

    def coarse(defect):
        for z in range(3):
            for b in range(8):
                if b < BANDS:
                    value = jnp.where(single, defect[b][z], 0.0)
                else:
                    value = jnp.zeros(plane, F32)
                for h in range(halves):
                    n = (z * halves + h) * size_x
                    cells_2[pl.ds(n * 8 + b, size_x, stride=8), :] = value[
                        :, h * LANES : (h + 1) * LANES
                    ]
        wide = jnp.concatenate(
            [cells_2[pl.ds(n * 8, 8), :] for n in range(count_2)], axis=1
        )
        partial = lax.dot_general(
            onehot[...],
            jnp.concatenate(split(wide), axis=0),
            (((1,), (1,)), ((), ())),
            preferred_element_type=F32,
        )
        partial = partial[:, :8] + partial[:, 8:16] + partial[:, 16:24]
        pairs = NAGG * BANDS // LANES
        acc = [jnp.zeros((8, LANES), F32)] * pairs
        for b in range(BANDS):
            column = jnp.broadcast_to(partial[:, b : b + 1], (NAGG, LANES))
            for i in range(NAGG // 8):
                for a in range(pairs):
                    acc[a] = (
                        acc[a]
                        + inverse_ref[b, pl.ds(i * 8, 8), a * LANES : (a + 1) * LANES]
                        * column[i * 8 : (i + 1) * 8]
                    )
        band = iota((8, LANES), 0)
        solved = jnp.zeros((8, LANES), F32)
        for a in range(pairs):
            both = jnp.broadcast_to(jnp.sum(acc[a], axis=0, keepdims=True), (8, LANES))
            solved = jnp.where(band == 2 * a, both, solved)
            solved = jnp.where(band == 2 * a + 1, pltpu.roll(both, NAGG, 1), solved)
        spread_out = jnp.dot(
            jnp.concatenate(split(solved[:, :NAGG]), axis=0), onehot[...], preferred_element_type=F32
        )
        spread_out = spread_out[:8] + spread_out[8:16] + spread_out[16:24]
        for n in range(count_2):
            cells_2[pl.ds(n * 8, 8), :] = spread_out[:, n * LANES : (n + 1) * LANES]

        def correction(b, z):
            parts = [
                cells_2[pl.ds(((z * halves + h) * size_x) * 8 + b, size_x, stride=8), :]
                for h in range(halves)
            ]
            return parts[0] if halves == 1 else jnp.concatenate(parts, axis=1)

        return correction

    def prolonged_sides():
        for x in range(2):
            for z in range(3):

                def neighbours(b):
                    mid = sums[x, z, b]
                    near_x = sums[1 - x, z, b]
                    if x == 0:
                        low_x, high_x = shifted(near_x, 1, 0, first_x), near_x
                    else:
                        low_x, high_x = near_x, shifted(near_x, -1, 0, last_x)
                    low_y, high_y = shifted(mid, ZQ, 1, first_y), shifted(mid, -ZQ, 1, last_y)
                    low_z = sums[x, z - 1, b] if z > 0 else shifted(sums[x, 2, b], 1, 1, first_z)
                    high_z = sums[x, z + 1, b] if z < 2 else shifted(sums[x, 0, b], -1, 1, last_z)
                    return [
                        [mid - low_x, mid - high_x],
                        [mid - low_y, mid - high_y],
                        [mid - low_z, mid - high_z],
                    ]

                acc = [None] * 3
                for b in range(BANDS):
                    differences = neighbours(b)
                    for d in range(3):
                        new = []
                        for a in range(BANDS):
                            c = coupling(d, a, b)
                            row = [c * value for value in differences[d]]
                            new.append(
                                row if b == 0 else [acc[d][a][i] + row[i] for i in range(2)]
                            )
                        acc[d] = new
                for d in range(3):
                    for side in range(2):
                        for a in range(BANDS):
                            sides[d, side, x, z, a] = acc[d][a][side]

    def over_x(body, carry):
        if not narrow:
            return lax.fori_loop(0, TX, body, carry)
        for x in range(TX):
            carry = body(x, carry)
        return carry

    def iteration(j, carry):
        factor = scale[...]

        def smooth(x, c_):
            columns = []
            for c in range(COMBOS):
                row = []
                for b in range(BANDS):
                    value = work[x, c, b] * factor
                    basis[j, x, c, b] = value
                    value = winv[x, c, b] * value
                    ext[x + 1, c, b] = value
                    row.append(value)
                mix_some(x, c, row, columns)
            return c_

        over_x(smooth, 0)
        ghosts()

        def down(x, c_):
            def finish(pair, cells, values):
                for b in range(BANDS):
                    defects = []
                    for n, (yt, zt) in enumerate(cells):
                        residual = basis[j, x, yt * ZT + zt, b]
                        defect = residual - values[b][n]
                        defects.append(defect)
                        work[x, yt * ZT + zt, b] = residual + defect
                    sums[x, pair, b] = (defects[0] + defects[1]) + (defects[2] + defects[3])

            operator_0(x, finish)
            return c_

        over_x(down, 0)

        for x in range(2):
            for z in range(3):
                for b in range(BANDS):
                    value = 0.125 * (sums[2 * x, z, b] + sums[2 * x + 1, z, b])
                    res_1[x, z, b] = value
                    cor_1[x, z, b] = winv_1[x, z, b] * value

        def defect_1(x, values):
            for b in range(BANDS):
                for z in range(3):
                    value = res_1[x, z, b] - values[b][z]
                    if x == 0:
                        sums[0, z, b] = value
                    else:
                        sums[0, z, b] = sums[0, z, b] + value

        operator_1(cor_1, defect_1)
        for b in range(BANDS):
            for z, value in enumerate(restrict_2([sums[0, z, b] for z in range(3)])):
                res_2[z, b] = value
                cor_2[z, b] = winv_2[z, b] * value
        values = operator_2(cor_2)
        correction = coarse(
            [[res_2[z, b] - values[b][z] for z in range(3)] for b in range(BANDS)]
        )
        for b in range(BANDS):
            for z in range(3):
                cor_2[z, b] = cor_2[z, b] + correction(b, z)
        values = operator_2(cor_2)
        for b in range(BANDS):
            e = [
                cor_2[z, b] + winv_2[z, b] * (res_2[z, b] - values[b][z]) for z in range(3)
            ]
            fine = [
                jnp.where(even_z, e[0], e[1]),
                jnp.where(even_z, e[0], e[2]),
                jnp.where(even_z, e[1], e[2]),
            ]
            for x in range(2):
                for z in range(3):
                    cor_1[x, z, b] = cor_1[x, z, b] + fine[z]

        def post_1(x, values):
            for b in range(BANDS):
                for z in range(3):
                    sums[x, z, b] = cor_1[x, z, b] + winv_1[x, z, b] * (
                        res_1[x, z, b] - values[b][z]
                    )

        operator_1(cor_1, post_1)

        if narrow:
            sides_of = mix_1(sums)
            for d in range(3):
                for x in range(2):
                    for z in range(3):
                        for a in range(BANDS):
                            mid, low, high = sides_of(d, a, x, z)
                            sides[d, 0, x, z, a] = low - mid
                            sides[d, 1, x, z, a] = high - mid
        else:
            prolonged_sides()

        def up(x, c_):
            columns = []
            for yt in range(YT):
                for zt in range(ZT):
                    z, c = zt // 2, yt * ZT + zt
                    row = []
                    for b in range(BANDS):
                        coarse_value = sums[x // 2, z, b]
                        applied = (
                            (sides[0, x % 2, x // 2, z, b] + sides[1, yt, x // 2, z, b])
                            + sides[2, zt % 2, x // 2, z, b]
                            + pots[x, c, b] * coarse_value
                        )
                        value = coarse_value + winv[x, c, b] * (work[x, c, b] - applied)
                        ext[x + 1, c, b] = value
                        row.append(value)
                    mix_some(x, c, row, columns)
            return c_

        over_x(up, 0)
        ghosts()

        def apply(x, parts):
            parts = list(parts)

            def finish(pair, cells, values):
                for b in range(BANDS):
                    for n, (yt, zt) in enumerate(cells):
                        c = yt * ZT + zt
                        fresh[x, c, b] = values[b][n]
                        for i in range(ITERS):
                            parts[i] = parts[i] + basis[i, x, c, b] * values[b][n]

            operator_0(x, finish)
            quarter = one_lane // GROUP
            for b in range(BANDS):
                for t in range(TILES):
                    merged = None
                    for i in range(4):
                        moved = pltpu.roll(
                            ext[x + 1, t * 4 + i, b], (GROUP * i + lanes - GROUP * my_y) % lanes, 1
                        )[:, :LANES]
                        merged = moved if i == 0 else jnp.where(quarter == i, moved, merged)
                    kept[j, x, b * TILES + t] = merged
            return tuple(parts)

        parts = over_x(apply, (jnp.zeros(plane, F32),) * ITERS)
        projections = [total_of(part) for part in parts]
        for i in range(ITERS):
            hess[i * ITERS + j] = projections[i]

        def subtract(x, parts):
            parts = list(parts)
            for c in range(COMBOS):
                for b in range(BANDS):
                    n = (c * BANDS + b) % 4
                    value = fresh[x, c, b]
                    for i in range(ITERS):
                        value = value - projections[i] * basis[i, x, c, b]
                    work[x, c, b] = value
                    parts[n] = parts[n] + value * value
            return tuple(parts)

        parts = lax.fori_loop(0, TX, subtract, (jnp.zeros(plane, F32),) * 4)
        total = (parts[0] + parts[1]) + (parts[2] + parts[3])
        norm = jnp.sqrt(total_of(total))
        hess[(j + 1) * ITERS + j] = norm
        scale[...] = 1.0 / norm
        return carry

    lax.fori_loop(0, ITERS, iteration, 0)

    h = [[hess[i * ITERS + j][:, :LANES] for j in range(ITERS)] for i in range(ITERS + 1)]
    normal = [
        [sum(h[i][j] * h[i][k] for i in range(ITERS + 1)) for k in range(ITERS)]
        for j in range(ITERS)
    ]
    first = beta[:, :LANES]
    weights = solve_small(normal, [first * h[0][j] for j in range(ITERS)], ITERS)

    for x in range(TX):
        for b in range(BANDS):
            for t in range(TILES):
                value = weights[0] * kept[0, x, b * TILES + t]
                for j in range(1, ITERS):
                    value = value + weights[j] * kept[j, x, b * TILES + t]
                value = pltpu.roll(value, (size_x - my_g) % size_x, 0)
                row = t * BANDS * TX + b * TX + x
                for z in range(VECS):
                    answer[z, row : row + 1, :] = value[z * groups : z * groups + 1]
    for k in range(VECS):
        outs[k][...] = answer[own ^ k]


def solve_small(normal_matrix, right_side, count):
    factor = {}
    for i in range(count):
        for k in range(i + 1):
            running = normal_matrix[i][k]
            for m in range(k):
                running = running - factor[i, m] * factor[k, m]
            if i == k:
                factor[i, i] = jnp.sqrt(running)
            else:
                factor[i, k] = running / factor[k, k]
    forward = []
    for i in range(count):
        running = right_side[i]
        for k in range(i):
            running = running - factor[i, k] * forward[k]
        forward.append(running / factor[i, i])
    answer = [None] * count
    for i in reversed(range(count)):
        running = forward[i]
        for k in range(i + 1, count):
            running = running - factor[k, i] * answer[k]
        answer[i] = running / factor[i, i]
    return answer


VMEM_SPEC = pl.BlockSpec(memory_space=pltpu.VMEM)
HBM_SPEC = pl.BlockSpec(memory_space=pltpu.HBM)
ANY_SPEC = pl.BlockSpec(memory_space=pl.ANY)
SMEM_SPEC = pl.BlockSpec(memory_space=pltpu.SMEM)


def bits(count):
    return count.bit_length() - 1


def shards(
    size_x, size_y, right_hand, region_labels, potential_table, coupling, aggregate_map,
    coarse_inverse,
):
    groups = size_x // VECS
    devices = size_x * size_y
    names = ("gx", "gy")
    stride = groups * size_y

    def exchanged(value, mask):
        return lax.ppermute(value, names, [(i, i ^ mask) for i in range(devices)])

    row_shape = jax.ShapeDtypeStruct((ROWS, LANES), F32)
    count = BANDS * TX
    packed = pl.pallas_call(
        functools.partial(pack_kernel, groups),
        out_shape=[row_shape] * VECS,
        in_specs=[HBM_SPEC] * 3,
        out_specs=[VMEM_SPEC] * VECS,
        scratch_shapes=[
            pltpu.VMEM((VECS * count + 8, CELLS), F32),
            pltpu.VMEM(right_hand.shape, F32),
            pltpu.VMEM(region_labels.shape, jnp.int32),
            pltpu.VMEM(aggregate_map.shape, jnp.int32),
            pltpu.SemaphoreType.DMA((3,)),
        ],
        compiler_params=pltpu.CompilerParams(vmem_limit_bytes=60 * 2**20),
        name="pack",
    )(right_hand, region_labels, aggregate_map)
    packed, coarse_inverse = lax.optimization_barrier((packed, coarse_inverse))
    turns = (0, 2, 3, 1)
    parts = [packed[0]] + [exchanged(packed[k], k * stride) for k in turns[1:]]
    inverse, permute = pl.pallas_call(
        order_kernel,
        out_shape=[
            jax.ShapeDtypeStruct((BANDS, NAGG, BANDS * NAGG), F32),
            jax.ShapeDtypeStruct((CELLS, CELLS), BF16),
        ],
        in_specs=[VMEM_SPEC],
        out_specs=[VMEM_SPEC] * 2,
        compiler_params=pltpu.CompilerParams(vmem_limit_bytes=16 * 2**20),
        cost_estimate=pl.CostEstimate(
            flops=6 * (NAGG * BANDS) ** 3, bytes_accessed=2**21, transcendentals=0
        ),
        name="order",
    )(coarse_inverse)

    steps = [("gy", i) for i in range(bits(size_y) - 1, 0, -1)]
    steps += [("gx", i) for i in range(bits(groups))]
    second, inverse = lax.optimization_barrier((jnp.stack(parts[2:]), inverse))
    halves = [[jnp.stack(parts[:2])], [second]]
    places = [[[(k, 0, 0) for k in turns[:2]]], [[(k, 0, 0) for k in turns[2:]]]]

    def widen(half, axis, bit):
        mask = 1 << bit
        sent = halves[half][0] if len(halves[half]) == 1 else jnp.concatenate(halves[half])
        halves[half].append(exchanged(sent, mask * (size_y if axis == "gx" else 1)))
        mask_g, mask_y = (mask, 0) if axis == "gx" else (0, mask)
        places[half].append(
            [(k, g ^ mask_g, y ^ mask_y) for blocks in places[half] for k, g, y in blocks]
        )

    for first, last in zip(steps, steps):
        widen(0, *first)
        widen(1, *last)
    widen(0, "gy", 0)
    widen(1, "gy", 0)
    pieces = halves[0] + halves[1]
    places = places[0] + places[1]

    lanes = size_y * GROUP
    plane = (size_x, lanes)
    count_2 = 3 * (lanes // LANES) * size_x
    narrow = plane == (SUBLANES, LANES)
    vmem = lambda *shape: pltpu.VMEM(shape + plane, F32)
    scratch = [
        pltpu.VMEM((ROWS * devices, LANES) if narrow else (ROWS, size_y, size_x, LANES), F32),
        vmem(ITERS, TX, COMBOS, BANDS),
        vmem(TX, COMBOS, BANDS),
        vmem(TX + 2, COMBOS, BANDS),
        vmem(TX, COMBOS, BANDS),
        vmem(TX, COMBOS, BANDS),
        vmem(TX, COMBOS, BANDS),
        vmem(TX, 3, BANDS),
        vmem(TX, COMBOS),
        vmem(3),
        pltpu.VMEM((NAGG, count_2 * LANES), BF16),
        vmem(2, 3, BANDS),
        vmem(2, 3, BANDS),
        vmem(3, BANDS),
        vmem(3, BANDS),
        vmem(3, 2, 2, 3, BANDS),
        pltpu.VMEM((MIXED, PARTS), F32),
        pltpu.VMEM((MIXED, PARTS), BF16),
        pltpu.VMEM((TX + 2, MIXED, COMBOS * LANES) if narrow else (8, LANES), F32),
        pltpu.VMEM((MIXED, 2 * TILES * LANES), F32),
        vmem(2, 3, BANDS),
        vmem(2, 3, BANDS),
        vmem(3, BANDS),
        vmem(3, BANDS),
        pltpu.VMEM((count_2 * 8, LANES), F32),
        pltpu.VMEM((ITERS, TX, BANDS * TILES, size_x, LANES), F32),
        vmem((ITERS + 1) * ITERS),
        vmem(),
        pltpu.VMEM((VECS, FIELD_ROWS, LANES), F32),
        pltpu.SemaphoreType.DMA((devices,)),
    ]
    held = sum(math.prod(ref.shape) * 4 for ref in scratch)
    answers = pl.pallas_call(
        functools.partial(solve_kernel, size_x, size_y, places),
        out_shape=[jax.ShapeDtypeStruct((FIELD_ROWS, LANES), F32)] * VECS,
        in_specs=[VMEM_SPEC if narrow else ANY_SPEC] * len(pieces) + [SMEM_SPEC, SMEM_SPEC, VMEM_SPEC],
        out_specs=[VMEM_SPEC] * VECS,
        scratch_shapes=scratch,
        compiler_params=pltpu.CompilerParams(
            vmem_limit_bytes=min(held + 6 * 2**20, 63 * 2**20)
        ),
        name="solve",
    )(*pieces, coupling, potential_table, inverse)
    received = [answers[0]] + [exchanged(answers[k], k * stride) for k in range(1, VECS)]
    return pl.pallas_call(
        functools.partial(unpack_kernel, groups),
        out_shape=jax.ShapeDtypeStruct(right_hand.shape, F32),
        in_specs=[VMEM_SPEC] * (VECS + 1),
        out_specs=VMEM_SPEC,
        scratch_shapes=[pltpu.VMEM((VECS * count, CELLS), F32)],
        compiler_params=pltpu.CompilerParams(vmem_limit_bytes=8 * 2**20),
        name="unpack",
    )(*received, permute)


def solution(mesh):
    return jax.shard_map(
        functools.partial(shards, mesh.shape["gx"], mesh.shape["gy"]),
        mesh=mesh,
        in_specs=(P(None, None, "gx", "gy"), P("gx", "gy"), P(), P(), P("gx", "gy"), P()),
        out_specs=P(None, None, "gx", "gy"),
        check_vma=False,
    )
```
